256 devices in a mesh: sub: 32 (over z, y), crow: 4 (over x_hi, core), ccol: 2 (over x_lo).
Axes of the slice: x: 4 (x_hi: 2, x_lo: 2; x = x_hi * 2 + x_lo), y: 4, z: 8, core: 2. Of those that a mesh axis runs over, the one named last changes fastest.
Arguments:
- load_cases: float32 [64, 1536, 256], P('sub', 'crow', 'ccol'), may hold values from -6 to 6
- stiffness: float32 [64, 1536, 1536], P('sub', 'crow'), may hold values from -1 to 6
- local_inverse: float32 [64, 1536, 1536], P('sub', 'crow'), may hold values from -1 to 1
- coarse_basis: float32 [64, 96, 1536], P('sub', None, 'crow'), may hold values from -0.15625 to 0.15625
- coarse_inverse: float32 [6144, 6144], P(('sub', 'crow')), may hold values from -1 to 3
- coupling: float32 [64, 6, 128, 128], P('sub'), may hold values from -0.5 to 0.5
- target_local_rows: int32 [64, 6, 128], P('sub'), may hold values from 0 to 1535
- neighbour_read_rows: int32 [64, 6, 128], P('sub'), may hold values from 0 to 1535
- neighbour: int32 [64, 6], P('sub'), may hold values from 0 to 63, as said below
- counts: int32 [64], P('sub'), may hold values from 1 to 6
Outputs:
- solution: float32 [64, 1536, 256], P('sub', 'crow', 'ccol')
- residual: float32 [64, 1536, 256], P('sub', 'crow', 'ccol')
The draws below stay inside these ranges and needn't reach their ends.
Inputs may be any that keep to these rules, and one draw needn't show every extreme that they name: neighbour[s, k] is a subdomain other than s, at most 2 away from s in the numbering. Only the first counts[s] interface blocks of subdomain s act. `target_local_rows`: rows may repeat within a block.
All inputs are finite; a program needn't handle non-finite values.
Results may differ from the reference program's by a relative error of at most 0.00013.
Values sent between devices are 32-bit elements; how exact they have to be, the bound alone decides.
A program may use at most 64 MiB of HBM per device.

```python
import math
import jax
import jax.numpy as jnp
from jax import lax

LOCAL_UNKNOWNS = 1536
NEV = 96
INTERFACE_ROWS = 128
SLOT_COUNT = 6
NEIGHBOUR_REACH = 2
ITERS = 2
SUBDOMAIN_COUNT = 64
NC = 6144
CASES = 256


def dominant(key, lead_shape, order_size, lower_end, upper_end, spread):
    key_diagonal, key_rest = jax.random.split(key)
    diagonal_part = jax.random.uniform(key_diagonal, lead_shape + (order_size,), jnp.float32, lower_end, upper_end)
    rest_reach = spread * math.sqrt(3.0 / order_size)
    rest_part = jax.random.uniform(key_rest, lead_shape + (order_size, order_size), jnp.float32, -rest_reach, rest_reach)
    return rest_part + diagonal_part[..., None] * jnp.eye(order_size, dtype=jnp.float32)


def draw_stiffness(key, part):
    return dominant(key, (SUBDOMAIN_COUNT,), LOCAL_UNKNOWNS, 2.0, 4.0, 1.0)


def draw_local_inverse(key, part):
    return dominant(key, (SUBDOMAIN_COUNT,), LOCAL_UNKNOWNS, 0.25, 0.5, 0.12)


def draw_coarse_inverse(key, part):
    return dominant(key, (), NC, 0.5, 1.5, 0.4)


def draw_neighbour(key, part):
    distance_key, side_key = jax.random.split(key)
    neighbour_distance = jax.random.randint(distance_key, (SUBDOMAIN_COUNT, SLOT_COUNT), 1, NEIGHBOUR_REACH + 1)
    sweep_direction = jax.random.randint(side_key, (SUBDOMAIN_COUNT, SLOT_COUNT), 0, 2) * 2 - 1
    own_index = jnp.arange(SUBDOMAIN_COUNT, dtype=jnp.int32)[:, None]
    candidate = own_index + neighbour_distance * sweep_direction
    outside = (candidate < 0) | (candidate >= SUBDOMAIN_COUNT)
    return jnp.where(outside, own_index - neighbour_distance * sweep_direction, candidate).astype(jnp.int32)


def place_ends(values, rng, low, top_value):
    shape = values.shape
    spot = [jax.random.randint(jax.random.fold_in(rng, axis), (), 0, shape[axis]) for axis in range(len(shape))]
    values = values.at[tuple(spot)].set(low)
    longest = shape.index(max(shape))
    spot[longest] = (spot[longest] + 1) % shape[longest]
    return values.at[tuple(spot)].set(top_value)


def levels(key, shape, cuts, low, high):
    factor_of = 1.0
    for position, blocks in cuts:
        steps = jax.random.uniform(jax.random.fold_in(jax.random.fold_in(key, 6), position), (blocks,), jnp.float32, low / len(cuts), high / len(cuts))
        factor_of = factor_of * jnp.repeat(jnp.exp(steps), shape[position] // blocks).reshape((-1,) + (1,) * (len(shape) - 1 - position))
    return factor_of


def normal_values(stream_key, shape, width, reach, pieces=(), held_as=jnp.bfloat16):
    drawn = jax.random.normal(stream_key, shape, jnp.float32) * width
    if len(pieces) > 0:
        drawn = levels(stream_key, shape, pieces, -0.22, 0.18) * drawn
    return jnp.clip(drawn, min=-reach, max=reach).astype(held_as)


def setup_inputs(seed: int = 0) -> dict:
    streams_of = jax.random.split(jax.random.key(seed), 11)
    load_cases = normal_values(streams_of[0], (SUBDOMAIN_COUNT, LOCAL_UNKNOWNS, CASES), 1.0, 6.0, ((0, 32), (1, 4), (2, 2)), jnp.float32)
    stiffness = draw_stiffness(jax.random.fold_in(streams_of[10], 71), 0)
    local_inverse = draw_local_inverse(jax.random.fold_in(streams_of[10], 71), 0)
    coarse_basis = normal_values(streams_of[3], (SUBDOMAIN_COUNT, NEV, LOCAL_UNKNOWNS), LOCAL_UNKNOWNS ** -0.5, 0.15625, ((0, 32), (2, 4)), jnp.float32)
    coarse_inverse = draw_coarse_inverse(jax.random.fold_in(streams_of[10], 71), 0)
    coupling = normal_values(streams_of[5], (SUBDOMAIN_COUNT, SLOT_COUNT, INTERFACE_ROWS, INTERFACE_ROWS), INTERFACE_ROWS ** -0.5, 0.5, ((0, 32),), jnp.float32)
    target_local_rows = place_ends(jax.random.randint(streams_of[6], (SUBDOMAIN_COUNT, SLOT_COUNT, INTERFACE_ROWS), 0, LOCAL_UNKNOWNS), jax.random.fold_in(streams_of[6], 1), 0, LOCAL_UNKNOWNS - 1).astype(jnp.int32)
    neighbour_read_rows = place_ends(jax.random.randint(streams_of[7], (SUBDOMAIN_COUNT, SLOT_COUNT, INTERFACE_ROWS), 0, LOCAL_UNKNOWNS), jax.random.fold_in(streams_of[7], 1), 0, LOCAL_UNKNOWNS - 1).astype(jnp.int32)
    neighbour = draw_neighbour(jax.random.fold_in(streams_of[10], 71), 0)
    counts = place_ends(jax.random.randint(streams_of[9], (SUBDOMAIN_COUNT,), 1, SLOT_COUNT + 1), jax.random.fold_in(streams_of[9], 1), 1, SLOT_COUNT).astype(jnp.int32)
    return dict(load_cases=load_cases, stiffness=stiffness, local_inverse=local_inverse, coarse_basis=coarse_basis, coarse_inverse=coarse_inverse, coupling=coupling, target_local_rows=target_local_rows, neighbour_read_rows=neighbour_read_rows, neighbour=neighbour, counts=counts)


damping = 0.7
highest_mode = lax.Precision.HIGHEST


def apply_operator(vector, stiffness, coupling, target_local_rows, neighbour_read_rows, neighbour, counts):
    local_part = jnp.einsum('slm,smc->slc', stiffness, vector, precision=highest_mode)
    sources = vector[neighbour[:, :, None], neighbour_read_rows]
    slot_terms = jnp.einsum('sknm,skmc->sknc', coupling, sources, precision=highest_mode)
    active_flag = (jnp.arange(SLOT_COUNT)[None, :] < counts[:, None]).astype(jnp.float32)
    slot_terms = slot_terms * active_flag[:, :, None, None]
    owners = jnp.broadcast_to(jnp.arange(SUBDOMAIN_COUNT)[:, None, None], target_local_rows.shape)
    inflow = jnp.zeros(vector.shape, jnp.float32).at[owners, target_local_rows].add(slot_terms)
    return local_part - inflow


def reference(load_cases, stiffness, local_inverse, coarse_basis, coarse_inverse, coupling, target_local_rows, neighbour_read_rows, neighbour, counts):
    solution = jnp.zeros_like(load_cases)
    residual = load_cases
    for sweep_index in range(ITERS):
        local_corr = jnp.einsum('slm,smc->slc', local_inverse, residual, precision=highest_mode)
        restricted = jnp.einsum('sel,slc->sec', coarse_basis, residual, precision=highest_mode)
        restricted = restricted.reshape(NC, CASES)
        coarse = jnp.dot(coarse_inverse, restricted, precision=highest_mode).reshape(SUBDOMAIN_COUNT, NEV, CASES)
        correction = local_corr + jnp.einsum('sel,sec->slc', coarse_basis, coarse, precision=highest_mode)
        solution = solution + damping * correction
        residual = residual - damping * apply_operator(correction, stiffness, coupling, target_local_rows, neighbour_read_rows, neighbour, counts)
    return solution, residual
```

```python
import jax
import jax.numpy as jnp
from jax import lax
from jax.experimental import pallas as pl
from jax.experimental.pallas import tpu as pltpu
from jax.sharding import Mesh
from jax.sharding import PartitionSpec as P

ITERS = 2
SUB = ("sub_0", "sub_1")
SUB_CROW = ("sub_0", "sub_1", "crow")
AXES = ("sub_0", "sub_1", "crow", "ccol")

damping = 0.7
f32 = jnp.float32
bf16 = jnp.bfloat16


def split(x):
    hi = x.astype(bf16)
    lo = (x - hi.astype(f32)).astype(bf16)
    return hi, lo


def wide(x):
    hi, lo = split(x)
    return jnp.concatenate([hi, lo], axis=1)


def mm(a, b):
    return jnp.dot(a, b, preferred_element_type=f32)


def quad(acc, rows):
    return acc[:rows, :128] + acc[:rows, 128:] + acc[rows:, :128]


def halves(acc):
    return acc[:, :128] + acc[:, 128:]


def kernel(
    r_hbm, s_hbm, l_hbm, b_hbm, k_hbm, c_hbm, lists, targets,
    sol, res,
    rb, lb, bf, bt, bo, am, stage, kst, km, rhs, xs, r1, part, pin, psend, precv,
    pickm, tt, ps, fr, tm, cst, cm, rl, co48, vsum,
    ldsem, ss, rs,
):
    z, y, cr, cc = [lax.axis_index(a) for a in AXES]
    co = lax.rem(cr, 2)
    oc = lax.rem(cr + 2, 4)
    sc = cr + 1 - 2 * co
    osc = lax.rem(sc + 2, 4)
    d = z * 4 + y
    d_up = lax.rem(d + 1, 32)
    d_dn = lax.rem(d + 31, 32)
    sib = (z, y, sc, cc)
    opp = (z, y, oc, cc)
    ops = (z, y, osc, cc)
    twin = (z, y, cr, 1 - cc)
    otwin = (z, y, oc, 1 - cc)
    up = (lax.div(d_up, 4), lax.rem(d_up, 4), cr, cc)
    dn = (lax.div(d_dn, 4), lax.rem(d_dn, 4), cr, cc)

    def yat(k):
        return (z, lax.rem(y + k, 4), cr, cc)

    def zat(k):
        return (lax.rem(z + k, 8), y, cr, cc)

    counter = [0]
    pending = []

    def remote(src, dst, dev, keep=True):
        i = counter[0]
        counter[0] += 1
        c = pltpu.make_async_remote_copy(
            src_ref=src, dst_ref=dst, send_sem=ss.at[i], recv_sem=rs.at[i],
            device_id=dev, device_id_type=pl.DeviceIdType.MESH,
        )
        if keep:
            pending.append(c)
        return c

    def load(i, src, dst):
        c = pltpu.make_async_copy(src, dst, ldsem.at[i])
        c.start()
        return c

    ld_b = load(0, b_hbm, bf.at[:, cr, pl.ds(0, 96)])
    ld_r = load(1, r_hbm, rb.at[0, :, cr])
    ld_l = [load(2 + s, l_hbm.at[s], stage.at[s]) for s in range(2)]
    ld_k = load(4, k_hbm, kst)
    ld_c = load(5, c_hbm.at[co], cst)

    bar = pltpu.get_barrier_semaphore()

    def greet(devs):
        for dev in devs:
            pl.semaphore_signal(bar, inc=1, device_id=dev, device_id_type=pl.DeviceIdType.MESH)

    greet([sib, opp, ops, twin, otwin, up, dn])

    @pl.when(co == 0)
    def _():
        greet([yat(1), yat(2), yat(3), zat(1), zat(7)])
        pl.semaphore_wait(bar, 12)

    @pl.when(co == 1)
    def _():
        greet([zat(k) for k in range(1, 8)] + [yat(1), yat(3)])
        pl.semaphore_wait(bar, 16)

    def conv_matrix(m, s):
        def body(i, carry):
            rows = pl.ds(pl.multiple_of(i * 32, 32), 32)
            rows2 = pl.ds(pl.multiple_of(384 + i * 32, 32), 32)
            hi, lo = split(stage[s, rows, :])
            am[m, s, rows, :] = hi
            am[m, s, rows2, :] = lo
            return carry
        lax.fori_loop(0, 12, body, 0)

    lane = lax.broadcasted_iota(jnp.int32, (128, 128), 1)
    sub_iota = lax.broadcasted_iota(jnp.int32, (128, 128), 0)

    def build_pick(m, row_of):
        def body(k, carry):
            row = jnp.broadcast_to(row_of(k), (128, 128))
            col = jnp.transpose(row)
            rows = pl.ds(pl.multiple_of(k * 128, 128), 128)
            for t in range(12):
                pickm[m, rows, 128 * t:128 * (t + 1)] = jnp.where(
                    col == lane + 128 * t, 1.0, 0.0
                ).astype(bf16)
            return carry
        lax.fori_loop(0, 6, body, 0)

    def build_scatter(s):
        for k in range(6):
            row = jnp.broadcast_to(targets[s, k:k + 1, :], (128, 128))

            def body(t, carry):
                rows = pl.ds(pl.multiple_of(t * 128, 128), 128)
                tt[s, rows, 128 * k:128 * (k + 1)] = jnp.where(
                    row == sub_iota + 128 * t, 1.0, 0.0
                ).astype(bf16)
                return carry
            lax.fori_loop(0, 12, body, 0)

    def build_bt(j):
        for s in range(2):
            t = jnp.transpose(bf[s, j])
            rows = pl.ds(pl.multiple_of(j * 384, 384), 384)
            bt[s, rows, :] = wide(t)

    def store_x(s, j, value):
        rows = pl.ds(pl.multiple_of(j * 384, 384), 384)
        xs[s, rows, :] = wide(value)

    def apply(m, s):
        return quad(mm(am[m, s], xs[s]), 384)

    def coarse_copies(it):
        q = {}
        g = rhs.at[it]
        first = counter[0]
        q["a1"] = [remote(g.at[z, y, 0], g.at[z, y, 0], yat(k), False) for k in (2, 1, 3)]
        q["f0"] = []

        def relay0(zz, h, dev):
            b = g.at[zz, pl.ds(2 * h, 2), 0]
            return remote(b, b, dev, False)

        q["p"] = {}
        q["m"] = {}
        for k in range(1, 5):
            for h in range(2):
                if k < 4 or h == 0:
                    q["p"][k, h] = relay0(lax.rem(z + 8 - (k - 1), 8), h, zat(1))
                if k < 4 or h == 1:
                    q["m"][k, h] = relay0(lax.rem(z + k - 1, 8), h, zat(7))
        zero_used = list(range(first, counter[0]))
        last0 = counter[0]
        counter[0] = first
        q["b1"] = [remote(g.at[z, y, 1], g.at[z, y, 1], zat(k), False) for k in (4, 3, 5, 2, 6, 1, 7)]

        def relay1(yy, h, dev):
            b = g.at[pl.ds(4 * h, 4), yy, 1]
            return remote(b, b, dev, False)

        q["u"] = {}
        q["v"] = {}
        for k in range(1, 3):
            for h in range(2):
                if k < 2 or h == 0:
                    q["u"][k, h] = relay1(lax.rem(y + 4 - (k - 1), 4), h, yat(1))
                if k < 2 or h == 1:
                    q["v"][k, h] = relay1(lax.rem(y + k - 1, 4), h, yat(3))
        counter[0] = max(last0, counter[0])

        def chip0(zz, lo, n):
            b = g.at[zz, pl.ds(lo, n), 0]
            return remote(b, b, sib, False)

        def chip1(lo, n, yy):
            b = g.at[pl.ds(lo, n), yy, 1]
            return remote(b, b, sib, False)

        q["f0own"] = chip0(z, 0, 4)
        q["f0p"] = {}
        q["f0m"] = {}
        for k in range(1, 5):
            for h in range(2):
                if k < 4 or h == 0:
                    q["f0p"][k, h] = chip0(lax.rem(z + 8 - k, 8), 2 * h, 2)
                if k < 4 or h == 1:
                    q["f0m"][k, h] = chip0(lax.rem(z + k, 8), 2 * h, 2)
        q["f1own"] = chip1(0, 8, y)
        q["f1u"] = {}
        q["f1v"] = {}
        for k in range(1, 3):
            for h in range(2):
                if k < 2 or h == 0:
                    q["f1u"][k, h] = chip1(4 * h, 4, lax.rem(y + 4 - k, 4))
                if k < 2 or h == 1:
                    q["f1v"][k, h] = chip1(4 * h, 4, lax.rem(y + k, 4))
        q["c0"] = q["a1"] + list(q["p"].values()) + list(q["m"].values()) + [q["f0own"]] + list(q["f0p"].values()) + list(q["f0m"].values())
        q["c1"] = q["b1"] + list(q["u"].values()) + list(q["v"].values()) + [q["f1own"]] + list(q["f1u"].values()) + list(q["f1v"].values())
        q["in0"] = [q["f0own"]] + list(q["f0p"].values()) + list(q["f0m"].values())
        q["in1"] = [q["f1own"]] + list(q["f1u"].values()) + list(q["f1v"].values())
        return q

    def coarse_step(q, n):
        @pl.when(co == 0)
        def _():
            if n == 0:
                for c in q["a1"]:
                    c.start()
            if n == 1:
                for c in q["a1"]:
                    c.wait_recv()
                for h in range(2):
                    q["p"][1, h].start()
                    q["m"][1, h].start()
                q["f0own"].start()
            if 2 <= n <= 5:
                k = n - 1
                for h in range(2):
                    for a, f in (("p", "f0p"), ("m", "f0m")):
                        if (k, h) in q[a]:
                            q[a][k, h].wait_recv()
                            if (k + 1, h) in q[a]:
                                q[a][k + 1, h].start()
                            q[f][k, h].start()
            if n == 5:
                for c in q["in1"]:
                    c.wait_recv()

        @pl.when(co == 1)
        def _():
            if n == 0:
                for c in q["b1"]:
                    c.start()
            if n == 2:
                for c in q["b1"]:
                    c.wait_recv()
                for h in range(2):
                    q["u"][1, h].start()
                    q["v"][1, h].start()
                q["f1own"].start()
            if 4 <= n <= 5:
                k = n - 3
                for h in range(2):
                    for a, f in (("u", "f1u"), ("v", "f1v")):
                        if (k, h) in q[a]:
                            q[a][k, h].wait_recv()
                            if (k + 1, h) in q[a]:
                                q[a][k + 1, h].start()
                            q[f][k, h].start()
            if n == 5:
                for c in q["in0"]:
                    c.wait_recv()

    def coarse_drain(q):
        @pl.when(co == 0)
        def _():
            for c in q["c0"]:
                c.wait_send()

        @pl.when(co == 1)
        def _():
            for c in q["c1"]:
                c.wait_send()

    def gather_copies(buf):
        g = {"own": [], "opp": [], "fwd": []}
        for s in range(2):
            g["own"].append(remote(buf.at[s, cr], buf.at[s, cr], sib))
            g["opp"].append(remote(buf.at[s, cr], buf.at[s, cr], opp))
            g["fwd"].append(remote(buf.at[s, oc], buf.at[s, oc], sib))
        return g

    def forward(g, s):
        g["opp"][s].wait_recv()
        g["fwd"][s].start()

    def arrived(g, s):
        g["own"][s].wait_recv()
        g["fwd"][s].wait_recv()

    def partial_restrict(it, own):
        for s in range(2):
            part[it, s] = quad(mm(bo[s], wide(own(s))), 96)
        c = remote(part.at[it, 1 - co], pin.at[it], sib)
        c.start()
        c.wait_recv()
        psend[it] = part[it, co] + pin[it]
        c2 = remote(psend.at[it], precv.at[it], opp)
        c2.start()
        return c2

    def coarse_solve(it):
        def body(i, acc):
            x = rhs[it, i].reshape(768, 128)
            cols = pl.ds(pl.multiple_of(i * 768, 768), 768)
            return acc + mm(km[:, cols], wide(x))
        acc = lax.fori_loop(0, 8, body, jnp.zeros((96, 256), f32))
        co48[it, cr] = quad(acc, 48)
        cs = [remote(co48.at[it, cr], co48.at[it, cr], dev) for dev in (opp, ops, sib)]
        for c in cs:
            c.start()
        return cs

    def rebuild(it, s):
        coarse = co48[it].reshape(2, 96, 128)[s]
        hi, lo = split(coarse)
        zero = jnp.zeros((32, 128), bf16)
        left = jnp.concatenate([hi, zero, hi, zero], axis=0)
        right = jnp.concatenate([lo, zero, jnp.zeros((128, 128), bf16)], axis=0)
        w = jnp.concatenate([left, right], axis=1)

        def body(j, carry):
            rows = pl.ds(pl.multiple_of(j * 384, 384), 384)
            v = lb[it, s, j] + halves(mm(bt[s, rows, :], w))
            xs[s, rows, :] = wide(v)
            return carry
        lax.fori_loop(0, 4, body, 0)
        rows = pl.ds(pl.multiple_of(cr * 384, 384), 384)
        v = lb[it, s, cr] + halves(mm(bt[s, rows, :], w))
        if it == 0:
            vsum[s] = v
        else:
            sol[s] = damping * (vsum[s] + v)

    def pick(m, s):
        return halves(mm(pickm[m], xs[s]))

    c_list_dn = remote(lists.at[co, pl.ds(0, 2)], rl.at[0], dn)
    c_list_up = remote(lists.at[co, pl.ds(2, 2)], rl.at[1], up)
    ld_b.wait()
    c_b1 = remote(bf.at[1 - cc, cr, pl.ds(0, 96)], bf.at[1 - cc, cr, pl.ds(0, 96)], otwin)
    c_b2 = remote(bf.at[cc, oc, pl.ds(0, 96)], bf.at[cc, oc, pl.ds(0, 96)], twin)
    c_bs = remote(bf.at[:, cr, pl.ds(0, 96)], bf.at[:, cr, pl.ds(0, 96)], sib)
    c_bo = remote(bf.at[:, oc, pl.ds(0, 96)], bf.at[:, oc, pl.ds(0, 96)], sib)
    c_b1.start()
    c_list_dn.start()
    c_list_up.start()
    for s in range(2):
        hi, lo = split(bf[s, cr, 0:96, :])
        bo[s, 0:96] = hi
        bo[s, 96:192] = lo
    ld_r.wait()
    gr = gather_copies(rb.at[0])
    c_part = partial_restrict(0, lambda s: rb[0, s, cr])
    for s in range(2):
        gr["opp"][s].start()
        gr["own"][s].start()
    c_bs.start()

    def zero_pad(j, carry):
        for s in range(2):
            bf[s, j, 96:128, :] = jnp.zeros((32, 384), f32)
        return carry
    lax.fori_loop(0, 4, zero_pad, 0)
    ld_l[0].wait()
    conv_matrix(0, 0)
    ld_s0 = load(6, s_hbm.at[0], stage.at[0])

    c_part.wait_recv()
    rhs[0, z, y, co] = psend[0] + precv[0]
    q = coarse_copies(0)
    coarse_step(q, 0)
    c_b1.wait_recv()
    c_b2.start()
    ld_l[1].wait()
    conv_matrix(0, 1)
    ld_s1 = load(7, s_hbm.at[1], stage.at[1])
    c_list_dn.wait_recv()
    c_list_up.wait_recv()
    coarse_step(q, 1)
    build_pick(0, lambda k: rl[0, 0, pl.ds(k, 1), :])
    coarse_step(q, 2)
    forward(gr, 0)
    build_pick(1, lambda k: rl[1, 0, pl.ds(k, 1), :])
    ld_k.wait()
    hi, lo = split(kst[...])
    km[0:48] = hi
    km[48:96] = lo
    coarse_step(q, 3)
    gl = gather_copies(lb.at[0])
    arrived(gr, 0)
    for j in range(4):
        store_x(0, j, rb[0, 0, j])
    lb[0, 0, cr] = apply(0, 0)
    gl["opp"][0].start()
    gl["own"][0].start()
    c_b2.wait_recv()
    c_bo.start()
    coarse_step(q, 4)
    forward(gr, 1)
    build_pick(2, lambda k: rl[co, 1, pl.ds(k, 1), :])
    arrived(gr, 1)
    for j in range(4):
        store_x(1, j, rb[0, 1, j])
    lb[0, 1, cr] = apply(0, 1)
    gl["opp"][1].start()
    gl["own"][1].start()
    coarse_step(q, 5)
    cs = coarse_solve(0)
    c_bs.wait_recv()
    c_bo.wait_recv()
    lax.fori_loop(0, 4, lambda j, carry: (build_bt(j), carry)[1], 0)
    forward(gl, 0)
    ld_s0.wait()
    conv_matrix(1, 0)
    ld_s1.wait()
    conv_matrix(1, 1)
    build_pick(3, lambda k: lists[co, 4, pl.ds(k, 1), :])
    build_scatter(0)
    build_scatter(1)
    ld_c.wait()
    for k in range(6):
        hi, lo = split(cst[k])
        cm[k, 0:128] = hi
        cm[k, 128:256] = lo

    for it in range(ITERS):
        for c in cs:
            c.wait_recv()
        arrived(gl, 0)
        rebuild(it, 0)
        ps[it, 1] = pick(1, 0)
        forward(gl, 1)
        arrived(gl, 1)
        rebuild(it, 1)
        ps[it, 0] = pick(0, 1)
        ps[it, co] = ps[it, co] + pick(2, co)
        c_up = remote(ps.at[it, 0], fr.at[it, 0], up)
        c_dn = remote(ps.at[it, 1], fr.at[it, 1], dn)
        c_up.start()
        c_dn.start()
        if it == 0:
            gy = gather_copies(rb.at[1])
        for s in range(2):
            if it == 0:
                rb[1, s, cr] = rb[0, s, cr] - damping * apply(1, s)
                gy["opp"][s].start()
                gy["own"][s].start()
            else:
                res[s] = r1[s] - damping * apply(1, s)
        own_rows = pick(3, 1 - co)
        if it == 0:
            forward(gy, 0)
        c_up.wait_recv()
        c_dn.wait_recv()
        src = own_rows + fr[it, 0] + fr[it, 1]
        for k in range(6):
            rows = slice(128 * k, 128 * (k + 1))
            tm[it, co, rows, :] = quad(mm(cm[k], wide(src[rows])), 128)
        c_tm = remote(tm.at[it, co], tm.at[it, co], sib)
        c_tm.start()
        if it == 0:
            forward(gy, 1)
        c_tm.wait_recv()
        tx = [wide(tm[it, s]) for s in range(2)]
        own = pl.ds(pl.multiple_of(cr * 384, 384), 384)
        for s in range(2):
            own_inflow = halves(mm(tt[s, own, :], tx[s]))
            if it == 0:
                r1[s] = rb[1, s, cr] + damping * own_inflow
                store_x(s, cr, r1[s])
            else:
                res[s] = res[s] + damping * own_inflow
        if it == 0:
            coarse_drain(q)
            c_part = partial_restrict(1, lambda s: r1[s])
            gl = gather_copies(lb.at[1])

            def fill(s):
                arrived(gy, s)

                def body(i, carry):
                    j = lax.rem(cr + i, 4)
                    rows = pl.ds(pl.multiple_of(j * 384, 384), 384)
                    v = rb[1, s, j] + damping * halves(mm(tt[s, rows, :], wide(tm[0, s])))
                    xs[s, rows, :] = wide(v)
                    return carry
                lax.fori_loop(1, 4, body, 0)

            fill(0)
            c_part.wait_recv()
            rhs[1, z, y, co] = psend[1] + precv[1]
            q = coarse_copies(1)
            coarse_step(q, 0)
            fill(1)
            lb[1, 0, cr] = apply(0, 0)
            gl["opp"][0].start()
            gl["own"][0].start()
            coarse_step(q, 1)
            lb[1, 1, cr] = apply(0, 1)
            gl["opp"][1].start()
            gl["own"][1].start()
            coarse_step(q, 2)
            coarse_step(q, 3)
            forward(gl, 0)
            coarse_step(q, 4)
            coarse_step(q, 5)
            cs = coarse_solve(1)
    coarse_drain(q)
    for c in pending:
        c.wait_send()


N_COPIES = 168


def per_device(
    load_cases,
    stiffness,
    local_inverse,
    coarse_basis,
    coarse_inverse,
    coupling,
    target_local_rows,
    neighbour_read_rows,
    neighbour,
    counts,
):
    d2 = lax.axis_index(SUB) * 2
    active = jnp.arange(6, dtype=jnp.int32)[None, :] < counts[:, None]
    near = jnp.where(active, neighbour, -9) - d2
    wanted = jnp.stack(
        [
            jnp.full((2,), -1, jnp.int32),
            jnp.full((2,), -2, jnp.int32),
            jnp.full((2,), 2, jnp.int32),
            jnp.full((2,), 3, jnp.int32),
            jnp.array([1, 0], jnp.int32),
        ],
        axis=1,
    )
    hit = (near[:, None, :] == wanted[:, :, None]) & active[:, None, :]
    lists = jnp.where(hit[:, :, :, None], neighbour_read_rows[:, None], -1)
    lists = jnp.pad(lists, ((0, 0), (0, 0), (0, 2), (0, 0)), constant_values=-1)
    any_spec = pl.BlockSpec(memory_space=pl.ANY)
    vmem = pl.BlockSpec(memory_space=pltpu.VMEM)
    block = jax.ShapeDtypeStruct((2, 384, 128), f32)
    V = pltpu.VMEM
    return pl.pallas_call(
        kernel,
        name="schwarz",
        out_shape=(block, block),
        in_specs=[any_spec] * 6 + [vmem] * 2,
        out_specs=(vmem, vmem),
        scratch_shapes=[
            V((2, 2, 4, 384, 128), f32),
            V((2, 2, 4, 384, 128), f32),
            V((2, 4, 128, 384), f32),
            V((2, 1536, 256), bf16),
            V((2, 192, 384), bf16),
            V((2, 2, 768, 1536), bf16),
            V((2, 384, 1536), f32),
            V((48, 6144), f32),
            V((96, 6144), bf16),
            V((2, 8, 4, 2, 96, 128), f32),
            V((2, 1536, 256), bf16),
            V((2, 384, 128), f32),
            V((2, 2, 96, 128), f32),
            V((2, 96, 128), f32),
            V((2, 96, 128), f32),
            V((2, 96, 128), f32),
            V((4, 768, 1536), bf16),
            V((2, 1536, 768), bf16),
            V((2, 2, 768, 128), f32),
            V((2, 2, 768, 128), f32),
            V((2, 2, 768, 128), f32),
            V((6, 128, 128), f32),
            V((6, 256, 128), bf16),
            V((2, 2, 8, 128), jnp.int32),
            V((2, 4, 48, 128), f32),
            V((2, 384, 128), f32),
            pltpu.SemaphoreType.DMA((8,)),
            pltpu.SemaphoreType.DMA((N_COPIES,)),
            pltpu.SemaphoreType.DMA((N_COPIES,)),
        ],
        compiler_params=pltpu.CompilerParams(
            collective_id=0, has_side_effects=True, vmem_limit_bytes=66_000_000
        ),
    )(
        load_cases, stiffness, local_inverse, coarse_basis, coarse_inverse, coupling,
        lists, target_local_rows,
    )


def solution(mesh):
    finer = Mesh(
        mesh.devices.reshape(8, 4, mesh.shape["crow"], mesh.shape["ccol"]),
        ("sub_0", "sub_1", "crow", "ccol"),
    )
    placed = (
        P(SUB, "crow", "ccol"),
        P(SUB, "crow", None),
        P(SUB, "crow", None),
        P(SUB, None, "crow"),
        P(SUB_CROW, None),
        P(SUB, None, None, None),
        P(SUB, None, None),
        P(SUB, None, None),
        P(SUB, None),
        P(SUB),
    )
    return jax.shard_map(
        per_device,
        mesh=finer,
        in_specs=placed,
        out_specs=(P(SUB, "crow", "ccol"), P(SUB, "crow", "ccol")),
        check_vma=False,
    )
```

```python
import jax
import jax.numpy as jnp
from jax import lax
from jax.experimental import pallas as pl
from jax.experimental.pallas import tpu as pltpu
from jax.sharding import Mesh
from jax.sharding import PartitionSpec as P

ITERS = 2
SUB = ("sub_0", "sub_1")
SUB_CROW = ("sub_0", "sub_1", "crow")
AXES = ("sub_0", "sub_1", "crow", "ccol")

damping = 0.7
f32 = jnp.float32
bf16 = jnp.bfloat16


def split(x):
    hi = x.astype(bf16)
    lo = (x - hi.astype(f32)).astype(bf16)
    return hi, lo


def wide(x):
    hi, lo = split(x)
    return jnp.concatenate([hi, lo], axis=1)


def mm(a, b):
    return jnp.dot(a, b, preferred_element_type=f32)


def quad(acc, rows):
    return acc[:rows, :128] + acc[:rows, 128:] + acc[rows:, :128]


def halves(acc):
    return acc[:, :128] + acc[:, 128:]


def kernel(
    r_hbm, s_hbm, l_hbm, b_hbm, k_hbm, c_hbm, t_hbm, rows_hbm, nbr_hbm, cnt_hbm,
    out,
    rb, lb, bf, bt, bo, bw, am, stage, kst, km, rhs, xs, r1, part, pin, psend, precv,
    pickm, qm, tt, ps, fr, tm, cst, cm, rl, co48, vsum, res,
    targets, read_rows, nbr, cnt, lists,
    ldsem, ss, rs,
):
    z, y, cr, cc = [lax.axis_index(a) for a in AXES]
    co = lax.rem(cr, 2)
    oc = lax.rem(cr + 2, 4)
    sc = cr + 1 - 2 * co
    osc = lax.rem(sc + 2, 4)
    d = z * 4 + y
    d_up = lax.rem(d + 1, 32)
    d_dn = lax.rem(d + 31, 32)
    sib = (z, y, sc, cc)
    opp = (z, y, oc, cc)
    ops = (z, y, osc, cc)
    twin = (z, y, cr, 1 - cc)
    otwin = (z, y, oc, 1 - cc)
    up = (lax.div(d_up, 4), lax.rem(d_up, 4), cr, cc)
    dn = (lax.div(d_dn, 4), lax.rem(d_dn, 4), cr, cc)

    def yat(k):
        return (z, lax.rem(y + k, 4), cr, cc)

    def zat(k):
        return (lax.rem(z + k, 8), y, cr, cc)

    counter = [0]
    pending = []

    def remote(src, dst, dev, keep=True):
        i = counter[0]
        counter[0] += 1
        c = pltpu.make_async_remote_copy(
            src_ref=src, dst_ref=dst, send_sem=ss.at[i], recv_sem=rs.at[i],
            device_id=dev, device_id_type=pl.DeviceIdType.MESH,
        )
        if keep:
            pending.append(c)
        return c

    def load(i, src, dst):
        c = pltpu.make_async_copy(src, dst, ldsem.at[i])
        c.start()
        return c

    ld_b = load(0, b_hbm, bf.at[:, cr, pl.ds(0, 96)])
    ld_r = load(1, r_hbm, rb.at[0, :, cr])
    ld_i = [
        load(8, t_hbm, targets),
        load(9, rows_hbm, read_rows),
        load(10, nbr_hbm, nbr),
        load(11, cnt_hbm, cnt),
    ]
    ld_l = [load(2 + s, l_hbm.at[s], stage.at[s]) for s in range(2)]
    ld_k = load(4, k_hbm, kst)
    ld_c = load(5, c_hbm.at[co], cst)

    bar = pltpu.get_barrier_semaphore()

    def greet(devs):
        for dev in devs:
            pl.semaphore_signal(bar, inc=1, device_id=dev, device_id_type=pl.DeviceIdType.MESH)

    greet([sib, opp, ops, twin, otwin, up, dn])

    @pl.when(co == 0)
    def _():
        greet([yat(1), yat(2), yat(3), zat(1), zat(7)])

    @pl.when(co == 1)
    def _():
        greet([zat(1), zat(7), yat(1), yat(3)])

    def conv_matrix(m, s):
        def body(i, carry):
            rows = pl.ds(pl.multiple_of(i * 32, 32), 32)
            rows2 = pl.ds(pl.multiple_of(384 + i * 32, 32), 32)
            hi, lo = split(stage[s, rows, :])
            am[m, s, rows, :] = hi
            am[m, s, rows2, :] = lo
            return carry
        lax.fori_loop(0, 12, body, 0)

    lane = lax.broadcasted_iota(jnp.int32, (128, 128), 1)
    sub_iota = lax.broadcasted_iota(jnp.int32, (128, 128), 0)

    def build_pick(m, row_of):
        def body(k, carry):
            row = jnp.broadcast_to(row_of(k), (128, 128))
            col = jnp.transpose(row)
            rows = pl.ds(pl.multiple_of(k * 128, 128), 128)
            for t in range(12):
                pickm[m, rows, 128 * t:128 * (t + 1)] = jnp.where(
                    col == lane + 128 * t, 1.0, 0.0
                ).astype(bf16)
            return carry
        lax.fori_loop(0, 6, body, 0)

    def build_scatter(s):
        for k in range(6):
            row = jnp.broadcast_to(targets[k, s:s + 1, :], (128, 128))

            def body(t, carry):
                rows = pl.ds(pl.multiple_of(t * 128, 128), 128)
                tt[s, rows, 128 * k:128 * (k + 1)] = jnp.where(
                    row == sub_iota + 128 * t, 1.0, 0.0
                ).astype(bf16)
                return carry
            lax.fori_loop(0, 12, body, 0)

    def build_bt(j):
        for s in range(2):
            t = jnp.transpose(bf[s, j])
            rows = pl.ds(pl.multiple_of(j * 384, 384), 384)
            bt[s, rows, :] = wide(t)

    def store_x(s, j, value):
        rows = pl.ds(pl.multiple_of(j * 384, 384), 384)
        xs[s, rows, :] = wide(value)

    def apply(m, s):
        return quad(mm(am[m, s], xs[s]), 384)

    def coarse_copies(it):
        q = {}
        g = rhs.at[it]
        first = counter[0]

        def block(zz, yy, half, dev):
            b = g.at[zz, yy, half]
            return remote(b, b, dev, False)

        def zm(k):
            return lax.rem(z + 8 + k, 8)

        def ym(k):
            return lax.rem(y + 4 + k, 4)

        for k in (1, 3, 2):
            q["y", k] = block(z, y, 0, yat(k))
        for j in range(4):
            for h in range(1, 5):
                if h < 4 or j < 2:
                    q["p", j, h] = block(zm(1 - h), ym(-j), 0, zat(1))
                if h < 4 or j >= 2:
                    q["m", j, h] = block(zm(h - 1), ym(-j), 0, zat(7))
        keys0 = list(q)
        last = counter[0]
        counter[0] = first
        for h in range(1, 5):
            q["s", h] = block(zm(1 - h), y, 1, zat(1))
            if h < 4:
                q["t", h] = block(zm(h - 1), y, 1, zat(7))
        for k in range(8):
            for h in range(1, 3):
                if h < 2 or k % 2 == 0:
                    q["u", k, h] = block(zm(-k), ym(1 - h), 1, yat(1))
                if h < 2 or k % 2 == 1:
                    q["v", k, h] = block(zm(-k), ym(h - 1), 1, yat(3))
        keys1 = [k for k in q if k not in keys0]
        counter[0] = max(last, counter[0])
        q["c0"] = [q[k] for k in keys0]
        q["c1"] = [q[k] for k in keys1]
        f0 = {}
        f0["y", 0] = block(z, y, 0, sib)
        for k in (1, 2, 3):
            f0["y", k] = block(z, ym(-k), 0, sib)
        for key in keys0:
            if key[0] == "p":
                f0[key] = block(zm(-key[2]), ym(-key[1]), 0, sib)
            if key[0] == "m":
                f0[key] = block(zm(key[2]), ym(-key[1]), 0, sib)
        f1 = {}
        f1["z", 0] = block(z, y, 1, sib)
        for k in range(1, 8):
            f1["z", k] = block(zm(-k), y, 1, sib)
        for key in keys1:
            if key[0] == "u":
                f1[key] = block(zm(-key[1]), ym(-key[2]), 1, sib)
            if key[0] == "v":
                f1[key] = block(zm(-key[1]), ym(key[2]), 1, sib)
        q["f0"] = f0
        q["f1"] = f1
        q["c0"] = q["c0"] + list(f0.values())
        q["c1"] = q["c1"] + list(f1.values())
        return q

    def coarse_step(q, n):
        def relay(f, a, b, j, hops):
            for h in hops:
                for way in (a, b):
                    if (way, j, h) in q:
                        q[way, j, h].wait_recv()
                        if (way, j, h + 1) in q:
                            q[way, j, h + 1].start()
                        f[way, j, h].start()

        @pl.when(co == 0)
        def _():
            f = q["f0"]

            def enter(k):
                q["y", k].wait_recv()
                q["p", k, 1].start()
                q["m", k, 1].start()
                f["y", k].start()

            if n == 0:
                for k in (1, 3, 2):
                    q["y", k].start()
                q["p", 0, 1].start()
                q["m", 0, 1].start()
                f["y", 0].start()
            if n == 1:
                relay(f, "p", "m", 0, [1])
                enter(1)
                enter(3)
            if n == 2:
                enter(2)
                relay(f, "p", "m", 0, [2])
            if 3 <= n <= 6:
                for j in (1, 3, 2):
                    relay(f, "p", "m", j, [n - 2])
                if n < 5:
                    relay(f, "p", "m", 0, [n])
            if n >= 7:
                for key, c in q["f1"].items():
                    if (key[1] == 4) == (n == 8):
                        c.wait_recv()

        @pl.when(co == 1)
        def _():
            f = q["f1"]

            def enter(h):
                for way, k in (("s", h), ("t", 8 - h)):
                    if (way, h) in q:
                        q[way, h].wait_recv()
                        if (way, h + 1) in q:
                            q[way, h + 1].start()
                        q["u", k, 1].start()
                        q["v", k, 1].start()
                        f["z", k].start()

            def both(h, hop):
                for k in sorted({h % 8, (8 - h) % 8}):
                    relay(f, "u", "v", k, [hop])

            if n == 0:
                q["s", 1].start()
                q["t", 1].start()
                q["u", 0, 1].start()
                q["v", 0, 1].start()
                f["z", 0].start()
            if 1 <= n <= 4:
                enter(n)
            if 1 <= n <= 5:
                both(n - 1, 1)
            if 2 <= n <= 6:
                both(n - 2, 2)
            if n >= 7:
                for key, c in q["f0"].items():
                    if (key[-1] == 4) == (n == 8):
                        c.wait_recv()

    def coarse_drain(q):
        @pl.when(co == 0)
        def _():
            for c in q["c0"]:
                c.wait_send()

        @pl.when(co == 1)
        def _():
            for c in q["c1"]:
                c.wait_send()

    def gather_copies(buf):
        g = {"own": [], "opp": [], "fwd": []}
        for s in range(2):
            g["own"].append(remote(buf.at[s, cr], buf.at[s, cr], sib))
            g["opp"].append(remote(buf.at[s, cr], buf.at[s, cr], opp))
            g["fwd"].append(remote(buf.at[s, oc], buf.at[s, oc], sib))
        return g

    def forward(g, s):
        g["opp"][s].wait_recv()
        g["fwd"][s].start()

    def arrived(g, s):
        g["own"][s].wait_recv()
        g["fwd"][s].wait_recv()

    def combine():
        c = remote(part.at[1 - co], pin, sib)
        c.start()
        c.wait_recv()
        psend[...] = part[co] + pin[...]
        c2 = remote(psend, precv, opp)
        c2.start()
        return c2

    def solve_group(it, off):
        i = lax.rem(z + off, 8)
        x = rhs[it, i].reshape(768, 128)
        cols = pl.ds(pl.multiple_of(i * 768, 768), 768)
        return mm(km[:, cols], wide(x))

    def solve_most(it):
        def body(i, acc):
            return acc + solve_group(it, i + lax.div(i, 4))
        return lax.fori_loop(0, 7, body, jnp.zeros((96, 256), f32))

    def solve_rest(it, acc):
        co48[it, cr] = quad(acc + solve_group(it, 4), 48)
        cs = [remote(co48.at[it, cr], co48.at[it, cr], dev) for dev in (opp, ops, sib)]
        for c in cs:
            c.start()
        return cs

    def weights(it, s):
        first = co48[it, pl.ds(2 * s, 2)].reshape(96, 128)
        hi, lo = split(first)
        zero = jnp.zeros((32, 128), bf16)
        left = jnp.concatenate([hi, zero, hi, zero], axis=0)
        right = jnp.concatenate([lo, zero, jnp.zeros((128, 128), bf16)], axis=0)
        return jnp.concatenate([left, right], axis=1)

    def rebuild(it, s):
        w = weights(it, s)

        def body(j, carry):
            rows = pl.ds(pl.multiple_of(j * 384, 384), 384)
            v = lb[it, s, j] + halves(mm(bt[s, rows, :], w))
            xs[s, rows, :] = wide(v)
            return carry
        lax.fori_loop(0, 4, body, 0)
        rows = pl.ds(pl.multiple_of(cr * 384, 384), 384)
        v = lb[it, s, cr] + halves(mm(bt[s, rows, :], w))
        if it == 0:
            vsum[s] = v
        else:
            out[0, s] = vsum[s] + v

    def pick(m, s, g):
        return halves(mm(pickm[m, 384 * g:384 * (g + 1)], xs[s]))

    ld_b.wait()
    for s in range(2):
        hi, lo = split(bf[s, cr, 0:96, :])
        bo[s, 0:96] = hi
        bo[s, 96:192] = lo
    ld_r.wait()
    for s in range(2):
        part[s] = quad(mm(bo[s], wide(rb[0, s, cr])), 96)
    for c in ld_i:
        c.wait()
    wanted = [-1, -2, 2, 3, 1 - co]
    for k in range(6):
        near = nbr[co, k] - 2 * d
        on = (cnt[co] > k).astype(jnp.int32)
        row = read_rows[k, pl.ds(co, 1), :]
        for a in range(5):
            h = (near == wanted[a]).astype(jnp.int32) * on
            lists[a, k:k + 1, :] = row * h + (h - 1)

    @pl.when(co == 0)
    def _():
        pl.semaphore_wait(bar, 12)

    @pl.when(co == 1)
    def _():
        pl.semaphore_wait(bar, 11)

    c_part = combine()
    c_list_dn = remote(lists.at[pl.ds(0, 2)], rl.at[0], dn)
    c_list_up = remote(lists.at[pl.ds(2, 2)], rl.at[1], up)
    c_b1 = remote(bf.at[1 - cc, cr, pl.ds(0, 96)], bf.at[1 - cc, cr, pl.ds(0, 96)], otwin)
    c_b2 = remote(bf.at[cc, oc, pl.ds(0, 96)], bf.at[cc, oc, pl.ds(0, 96)], twin)
    c_bs = remote(bf.at[:, cr, pl.ds(0, 96)], bf.at[:, cr, pl.ds(0, 96)], sib)
    c_bo = remote(bf.at[:, oc, pl.ds(0, 96)], bf.at[:, oc, pl.ds(0, 96)], sib)
    c_b1.start()
    gr = gather_copies(rb.at[0])
    for s in range(2):
        gr["opp"][s].start()
        gr["own"][s].start()
    c_list_dn.start()
    c_list_up.start()
    c_bs.start()

    def zero_pad(j, carry):
        for s in range(2):
            bf[s, j, 96:128, :] = jnp.zeros((32, 384), f32)
        return carry
    lax.fori_loop(0, 4, zero_pad, 0)
    ld_l[0].wait()
    conv_matrix(0, 0)
    ld_s0 = load(6, s_hbm.at[0], stage.at[0])
    ld_l[1].wait()
    conv_matrix(0, 1)
    ld_s1 = load(7, s_hbm.at[1], stage.at[1])

    c_part.wait_recv()
    rhs[0, z, y, co] = psend[...] + precv[...]
    q = coarse_copies(0)
    coarse_step(q, 0)
    ld_k.wait()
    hi, lo = split(kst[...])
    km[0:48] = hi
    km[48:96] = lo
    c_list_dn.wait_recv()
    c_list_up.wait_recv()
    build_pick(0, lambda k: rl[0, 0, pl.ds(k, 1), :])
    coarse_step(q, 1)
    build_pick(1, lambda k: rl[1, 0, pl.ds(k, 1), :])
    coarse_step(q, 2)
    forward(gr, 0)
    build_scatter(0)
    coarse_step(q, 3)
    gl = gather_copies(lb.at[0])
    arrived(gr, 0)
    for j in range(4):
        store_x(0, j, rb[0, 0, j])
    lb[0, 0, cr] = apply(0, 0)
    gl["opp"][0].start()
    gl["own"][0].start()
    coarse_step(q, 4)
    c_b1.wait_recv()
    c_b2.start()
    build_pick(2, lambda k: rl[co, 1, pl.ds(k, 1), :])
    coarse_step(q, 5)
    forward(gr, 1)
    arrived(gr, 1)
    for j in range(4):
        store_x(1, j, rb[0, 1, j])
    lb[0, 1, cr] = apply(0, 1)
    gl["opp"][1].start()
    gl["own"][1].start()
    coarse_step(q, 7)
    acc = solve_most(0)
    coarse_step(q, 6)
    coarse_step(q, 8)
    cs = solve_rest(0, acc)
    c_b2.wait_recv()
    c_bo.start()
    ld_s0.wait()
    conv_matrix(1, 0)
    ld_s1.wait()
    conv_matrix(1, 1)
    build_pick(3, lambda k: lists[4, pl.ds(k, 1), :])
    forward(gl, 0)
    build_scatter(1)
    c_bs.wait_recv()
    c_bo.wait_recv()
    lax.fori_loop(0, 4, lambda j, carry: (build_bt(j), carry)[1], 0)
    for j in range(4):
        hi, lo = split(bf[co, j, 0:96, :])
        bw[0:96, 384 * j:384 * (j + 1)] = hi
        bw[96:192, 384 * j:384 * (j + 1)] = lo
    ld_c.wait()
    for k in range(6):
        hi, lo = split(cst[k])
        cm[k, 0:128] = hi
        cm[k, 128:256] = lo

    for it in range(ITERS):
        c_up = []
        c_dn = []
        for g in range(2):
            part_rows = pl.ds(384 * g, 384)
            c_up.append(remote(ps.at[it, 0, part_rows], fr.at[it, 0, part_rows], up))
            c_dn.append(remote(ps.at[it, 1, part_rows], fr.at[it, 1, part_rows], dn))
        if it == 1:
            for s in range(2):
                arrived(gl, s)
                for j in range(4):
                    store_x(s, j, lb[1, s, j])
            for g in range(2):
                rows = slice(384 * g, 384 * (g + 1))
                ps[1, 1, rows] = pick(1, 0, g)
                ps[1, 0, rows] = pick(0, 1, g)
                ps[1, co, rows] = ps[1, co, rows] + pick(2, co, g)
            for c in cs:
                c.wait_recv()
            ws = [weights(1, 1), weights(1, 0), weights(1, co)]
            for g in range(2):
                rows = slice(384 * g, 384 * (g + 1))
                for m, dest in ((0, 0), (1, 1), (2, co)):
                    ps[1, dest, rows] = ps[1, dest, rows] + halves(mm(qm[m, rows], ws[m]))
                c_up[g].start()
                c_dn[g].start()
            rebuild(1, 0)
            rebuild(1, 1)
        if it == 0:
            for c in cs:
                c.wait_recv()
            arrived(gl, 0)
            rebuild(0, 0)
            for g in range(2):
                rows = slice(384 * g, 384 * (g + 1))
                ps[0, 1, rows] = pick(1, 0, g)

                @pl.when(co == 0)
                def _():
                    c_dn[g].start()
            forward(gl, 1)
            arrived(gl, 1)
            rebuild(0, 1)
            for g in range(2):
                rows = slice(384 * g, 384 * (g + 1))
                ps[0, 0, rows] = pick(0, 1, g)

                @pl.when(co == 1)
                def _():
                    c_up[g].start()
                ps[0, co, rows] = ps[0, co, rows] + pick(2, co, g)

                @pl.when(co == 0)
                def _():
                    c_up[g].start()

                @pl.when(co == 1)
                def _():
                    c_dn[g].start()
        if it == 0:
            gy = gather_copies(rb.at[1])
        for s in range(2):
            if it == 0:
                rb[1, s, cr] = rb[0, s, cr] - damping * apply(1, s)
                gy["opp"][s].start()
                gy["own"][s].start()
            else:
                res[s] = r1[s] - damping * apply(1, s)
        own_rows = [pick(3, 1 - co, g) for g in range(2)]
        c_tm = []
        for g in range(2):
            if it == 0:
                for m, src_s in ((0, 1), (1, 0)) if g == 0 else ((2, co),):
                    for h in range(2):
                        rows = slice(384 * h, 384 * (h + 1))
                        qm[m, rows] = mm(pickm[m, rows], bt[src_s]).astype(bf16)
            c_up[g].wait_recv()
            c_dn[g].wait_recv()
            part_rows = pl.ds(384 * g, 384)
            src = own_rows[g] + fr[it, 0, part_rows] + fr[it, 1, part_rows]
            for k in range(3):
                rows = slice(384 * g + 128 * k, 384 * g + 128 * (k + 1))
                tm[it, co, rows, :] = quad(
                    mm(cm[3 * g + k], wide(src[128 * k:128 * (k + 1)])), 128
                )
            c = remote(tm.at[it, co, part_rows], tm.at[it, co, part_rows], sib)
            c.start()
            c_tm.append(c)
            if it == 0:
                forward(gy, g)
        for c in c_tm:
            c.wait_recv()
        tx = [wide(tm[it, s]) for s in range(2)]
        own = pl.ds(pl.multiple_of(cr * 384, 384), 384)
        for s in range(2):
            own_inflow = halves(mm(tt[s, own, :], tx[s]))
            if it == 0:
                r1[s] = rb[1, s, cr] + damping * own_inflow
                store_x(s, cr, r1[s])
            else:
                out[1, s] = 0.5 * (res[s] + damping * own_inflow)
        if it == 0:
            coarse_drain(q)
            gl = gather_copies(lb.at[1])

            def fill(s):
                def body(i, carry):
                    j = lax.rem(cr + i, 4)
                    rows = pl.ds(pl.multiple_of(j * 384, 384), 384)
                    v = rb[1, s, j] + damping * halves(mm(tt[s, rows, :], wide(tm[0, s])))
                    xs[s, rows, :] = wide(v)
                    return carry
                lax.fori_loop(1, 4, body, 0)

            arrived(gy, 0)
            arrived(gy, 1)
            fill(co)
            rhs[1, z, y, co] = quad(mm(bw[...], xs[co]), 96)
            q = coarse_copies(1)
            coarse_step(q, 0)
            fill(1 - co)
            coarse_step(q, 1)
            lb[1, 0, cr] = apply(0, 0)
            gl["opp"][0].start()
            gl["own"][0].start()
            coarse_step(q, 2)
            lb[1, 1, cr] = apply(0, 1)
            gl["opp"][1].start()
            gl["own"][1].start()
            for n in range(3, 6):
                coarse_step(q, n)
            forward(gl, 0)
            coarse_step(q, 7)
            acc = solve_most(1)
            coarse_step(q, 6)
            forward(gl, 1)
            coarse_step(q, 8)
            cs = solve_rest(1, acc)
    coarse_drain(q)
    for c in pending:
        c.wait_send()


N_COPIES = 260


def per_device(
    load_cases,
    stiffness,
    local_inverse,
    coarse_basis,
    coarse_inverse,
    coupling,
    target_local_rows,
    neighbour_read_rows,
    neighbour,
    counts,
):
    any_spec = pl.BlockSpec(memory_space=pl.ANY)
    vmem = pl.BlockSpec(memory_space=pltpu.VMEM)
    V = pltpu.VMEM
    both = pl.pallas_call(
        kernel,
        name="schwarz",
        out_shape=jax.ShapeDtypeStruct((2, 2, 384, 128), f32),
        in_specs=[any_spec] * 10,
        out_specs=vmem,
        scratch_shapes=[
            V((2, 2, 4, 384, 128), f32),
            V((2, 2, 4, 384, 128), f32),
            V((2, 4, 128, 384), f32),
            V((2, 1536, 256), bf16),
            V((2, 192, 384), bf16),
            V((192, 1536), bf16),
            V((2, 2, 768, 1536), bf16),
            V((2, 384, 1536), f32),
            V((48, 6144), f32),
            V((96, 6144), bf16),
            V((2, 8, 4, 2, 96, 128), f32),
            V((2, 1536, 256), bf16),
            V((2, 384, 128), f32),
            V((2, 96, 128), f32),
            V((96, 128), f32),
            V((96, 128), f32),
            V((96, 128), f32),
            V((4, 768, 1536), bf16),
            V((3, 768, 256), bf16),
            V((2, 1536, 768), bf16),
            V((2, 2, 768, 128), f32),
            V((2, 2, 768, 128), f32),
            V((2, 2, 768, 128), f32),
            V((6, 128, 128), f32),
            V((6, 256, 128), bf16),
            V((2, 2, 8, 128), jnp.int32),
            V((2, 4, 48, 128), f32),
            V((2, 384, 128), f32),
            V((2, 384, 128), f32),
            V((6, 2, 128), jnp.int32),
            V((6, 2, 128), jnp.int32),
            pltpu.SMEM((2, 6), jnp.int32),
            pltpu.SMEM((2,), jnp.int32),
            V((5, 8, 128), jnp.int32),
            pltpu.SemaphoreType.DMA((12,)),
            pltpu.SemaphoreType.DMA((N_COPIES,)),
            pltpu.SemaphoreType.DMA((N_COPIES,)),
        ],
        compiler_params=pltpu.CompilerParams(
            collective_id=0, has_side_effects=True, vmem_limit_bytes=66_000_000
        ),
    )(
        load_cases, stiffness, local_inverse, coarse_basis, coarse_inverse, coupling,
        target_local_rows.transpose(1, 0, 2), neighbour_read_rows.transpose(1, 0, 2),
        neighbour, counts,
    )
    return damping * both[0], 2.0 * both[1]


def solution(mesh):
    finer = Mesh(
        mesh.devices.reshape(8, 4, mesh.shape["crow"], mesh.shape["ccol"]),
        ("sub_0", "sub_1", "crow", "ccol"),
    )
    placed = (
        P(SUB, "crow", "ccol"),
        P(SUB, "crow", None),
        P(SUB, "crow", None),
        P(SUB, None, "crow"),
        P(SUB_CROW, None),
        P(SUB, None, None, None),
        P(SUB, None, None),
        P(SUB, None, None),
        P(SUB, None),
        P(SUB),
    )
    return jax.shard_map(
        per_device,
        mesh=finer,
        in_specs=placed,
        out_specs=(P(SUB, "crow", "ccol"), P(SUB, "crow", "ccol")),
        check_vma=False,
    )
```

```python
import jax
import jax.numpy as jnp
from jax import lax
from jax.experimental import pallas as pl
from jax.experimental.pallas import tpu as pltpu
from jax.sharding import Mesh
from jax.sharding import PartitionSpec as P

ITERS = 2
SUB = ("sub_0", "sub_1")
SUB_CROW = ("sub_0", "sub_1", "crow")
AXES = ("sub_0", "sub_1", "crow", "ccol")

damping = 0.7
f32 = jnp.float32
bf16 = jnp.bfloat16


def split(x):
    hi = x.astype(bf16)
    lo = (x - hi.astype(f32)).astype(bf16)
    return hi, lo


def wide(x):
    hi, lo = split(x)
    return jnp.concatenate([hi, lo], axis=1)


def mm(a, b):
    return jnp.dot(a, b, preferred_element_type=f32)


def quad(acc, rows):
    return acc[:rows, :128] + acc[:rows, 128:] + acc[rows:, :128]


def halves(acc):
    return acc[:, :128] + acc[:, 128:]


def kernel(
    r_hbm, s_hbm, l_hbm, b_hbm, k_hbm, c_hbm, t_hbm, rows_hbm, nbr_hbm, cnt_hbm,
    out,
    rb, lb, bf, bt, bo, bw, am, stage, kst, km, rhs, xs, r1, part, pin,
    pickm, qm, tt, ps, fr, tm, cst, cm, rl, co48, vsum, res,
    targets, read_rows, nbr, cnt, lists,
    ldsem, ss, rs,
):
    z, y, cr, cc = [lax.axis_index(a) for a in AXES]
    co = lax.rem(cr, 2)
    oc = lax.rem(cr + 2, 4)
    sc = cr + 1 - 2 * co
    osc = lax.rem(sc + 2, 4)
    d = z * 4 + y
    d_up = lax.rem(d + 1, 32)
    d_dn = lax.rem(d + 31, 32)
    sib = (z, y, sc, cc)
    opp = (z, y, oc, cc)
    ops = (z, y, osc, cc)
    twin = (z, y, cr, 1 - cc)
    otwin = (z, y, oc, 1 - cc)
    up = (lax.div(d_up, 4), lax.rem(d_up, 4), cr, cc)
    dn = (lax.div(d_dn, 4), lax.rem(d_dn, 4), cr, cc)

    def yat(k):
        return (z, lax.rem(y + k, 4), cr, cc)

    def zat(k):
        return (lax.rem(z + k, 8), y, cr, cc)

    counter = [0]
    pending = []

    def remote(src, dst, dev, keep=True):
        i = counter[0]
        counter[0] += 1
        c = pltpu.make_async_remote_copy(
            src_ref=src, dst_ref=dst, send_sem=ss.at[i], recv_sem=rs.at[i],
            device_id=dev, device_id_type=pl.DeviceIdType.MESH,
        )
        if keep:
            pending.append(c)
        return c

    def load(i, src, dst):
        c = pltpu.make_async_copy(src, dst, ldsem.at[i])
        c.start()
        return c

    ld_b = load(0, b_hbm, bf.at[:, cr, pl.ds(0, 96)])
    ld_r = load(1, r_hbm, rb.at[0, :, cr])
    ld_i = [
        load(8, t_hbm, targets),
        load(9, rows_hbm, read_rows),
        load(10, nbr_hbm, nbr),
        load(11, cnt_hbm, cnt),
    ]
    ld_l = [load(2 + s, l_hbm.at[s], stage.at[s]) for s in range(2)]
    ld_k = load(4, k_hbm, kst)
    ld_c = load(5, c_hbm.at[co], cst)

    bar = pltpu.get_barrier_semaphore()

    def greet(devs):
        for dev in devs:
            pl.semaphore_signal(bar, inc=1, device_id=dev, device_id_type=pl.DeviceIdType.MESH)

    greet([sib, opp, ops, twin, otwin, up, dn])

    @pl.when(co == 0)
    def _():
        greet([yat(1), yat(2), yat(3), zat(1), zat(7)])

    @pl.when(co == 1)
    def _():
        greet([zat(1), zat(7), yat(1), yat(3)])

    def conv_matrix(m, s):
        def body(i, carry):
            rows = pl.ds(pl.multiple_of(i * 32, 32), 32)
            rows2 = pl.ds(pl.multiple_of(384 + i * 32, 32), 32)
            hi, lo = split(stage[s, rows, :])
            am[m, s, rows, :] = hi
            am[m, s, rows2, :] = lo
            return carry
        lax.fori_loop(0, 12, body, 0)

    lane = lax.broadcasted_iota(jnp.int32, (128, 128), 1)
    sub_iota = lax.broadcasted_iota(jnp.int32, (128, 128), 0)

    def build_pick(m, row_of):
        def body(k, carry):
            row = jnp.broadcast_to(row_of(k), (128, 128))
            col = jnp.transpose(row)
            rows = pl.ds(pl.multiple_of(k * 128, 128), 128)
            for t in range(12):
                pickm[m, rows, 128 * t:128 * (t + 1)] = jnp.where(
                    col == lane + 128 * t, 1.0, 0.0
                ).astype(bf16)
            return carry
        lax.fori_loop(0, 6, body, 0)

    def build_scatter(s):
        for k in range(6):
            row = jnp.broadcast_to(targets[k, s:s + 1, :], (128, 128))

            def body(t, carry):
                rows = pl.ds(pl.multiple_of(t * 128, 128), 128)
                tt[s, rows, 128 * k:128 * (k + 1)] = jnp.where(
                    row == sub_iota + 128 * t, 1.0, 0.0
                ).astype(bf16)
                return carry
            lax.fori_loop(0, 12, body, 0)

    def build_bt(j):
        for s in range(2):
            t = jnp.transpose(bf[s, j])
            rows = pl.ds(pl.multiple_of(j * 384, 384), 384)
            bt[s, rows, :] = wide(t)

    def store_x(s, j, value):
        rows = pl.ds(pl.multiple_of(j * 384, 384), 384)
        xs[s, rows, :] = wide(value)

    def apply(m, s):
        return quad(mm(am[m, s], xs[s]), 384)

    def coarse_copies(it):
        q = {}
        g = rhs.at[it]
        first = counter[0]

        def block(zz, yy, half, dev):
            b = g.at[zz, yy, half]
            return remote(b, b, dev, False)

        def zm(k):
            return lax.rem(z + 8 + k, 8)

        def ym(k):
            return lax.rem(y + 4 + k, 4)

        for k in (1, 3, 2):
            q["y", k] = block(z, y, 0, yat(k))
        for j in range(4):
            for h in range(1, 5):
                if h < 4 or j < 2:
                    q["p", j, h] = block(zm(1 - h), ym(-j), 0, zat(1))
                if h < 4 or j >= 2:
                    q["m", j, h] = block(zm(h - 1), ym(-j), 0, zat(7))
        keys0 = list(q)
        last = counter[0]
        counter[0] = first
        for h in range(1, 5):
            q["s", h] = block(zm(1 - h), y, 1, zat(1))
            if h < 4:
                q["t", h] = block(zm(h - 1), y, 1, zat(7))
        for k in range(8):
            for h in range(1, 3):
                if h < 2 or k % 2 == 0:
                    q["u", k, h] = block(zm(-k), ym(1 - h), 1, yat(1))
                if h < 2 or k % 2 == 1:
                    q["v", k, h] = block(zm(-k), ym(h - 1), 1, yat(3))
        keys1 = [k for k in q if k not in keys0]
        counter[0] = max(last, counter[0])
        q["c0"] = [q[k] for k in keys0]
        q["c1"] = [q[k] for k in keys1]
        f0 = {}
        f0["y", 0] = block(z, y, 0, sib)
        for k in (1, 2, 3):
            f0["y", k] = block(z, ym(-k), 0, sib)
        for key in keys0:
            if key[0] == "p":
                f0[key] = block(zm(-key[2]), ym(-key[1]), 0, sib)
            if key[0] == "m":
                f0[key] = block(zm(key[2]), ym(-key[1]), 0, sib)
        f1 = {}
        f1["z", 0] = block(z, y, 1, sib)
        for k in range(1, 8):
            f1["z", k] = block(zm(-k), y, 1, sib)
        for key in keys1:
            if key[0] == "u":
                f1[key] = block(zm(-key[1]), ym(-key[2]), 1, sib)
            if key[0] == "v":
                f1[key] = block(zm(-key[1]), ym(key[2]), 1, sib)
        q["f0"] = f0
        q["f1"] = f1
        q["c0"] = q["c0"] + list(f0.values())
        q["c1"] = q["c1"] + list(f1.values())
        return q

    def coarse_step(q, n):
        def relay(f, a, b, j, hops):
            for h in hops:
                for way in (a, b):
                    if (way, j, h) in q:
                        q[way, j, h].wait_recv()
                        if (way, j, h + 1) in q:
                            q[way, j, h + 1].start()
                        f[way, j, h].start()

        @pl.when(co == 0)
        def _():
            f = q["f0"]

            def enter(k):
                q["y", k].wait_recv()
                q["p", k, 1].start()
                q["m", k, 1].start()
                f["y", k].start()

            if n == 0:
                for k in (1, 3, 2):
                    q["y", k].start()
                q["p", 0, 1].start()
                q["m", 0, 1].start()
                f["y", 0].start()
            if n == 1:
                relay(f, "p", "m", 0, [1])
                enter(1)
                enter(3)
            if n == 2:
                enter(2)
                relay(f, "p", "m", 0, [2])
            if 3 <= n <= 6:
                for j in (1, 3, 2):
                    relay(f, "p", "m", j, [n - 2])
                if n < 5:
                    relay(f, "p", "m", 0, [n])
            if n >= 7:
                for key, c in q["f1"].items():
                    if (key[1] == 4) == (n == 8):
                        c.wait_recv()

        @pl.when(co == 1)
        def _():
            f = q["f1"]

            def enter(h):
                for way, k in (("s", h), ("t", 8 - h)):
                    if (way, h) in q:
                        q[way, h].wait_recv()
                        if (way, h + 1) in q:
                            q[way, h + 1].start()
                        q["u", k, 1].start()
                        q["v", k, 1].start()
                        f["z", k].start()

            def both(h, hop):
                for k in sorted({h % 8, (8 - h) % 8}):
                    relay(f, "u", "v", k, [hop])

            if n == 0:
                q["s", 1].start()
                q["t", 1].start()
                q["u", 0, 1].start()
                q["v", 0, 1].start()
                f["z", 0].start()
            if 1 <= n <= 4:
                enter(n)
            if 1 <= n <= 5:
                both(n - 1, 1)
            if 2 <= n <= 6:
                both(n - 2, 2)
            if n >= 7:
                for key, c in q["f0"].items():
                    if (key[-1] == 4) == (n == 8):
                        c.wait_recv()

    def coarse_drain(q):
        @pl.when(co == 0)
        def _():
            for c in q["c0"]:
                c.wait_send()

        @pl.when(co == 1)
        def _():
            for c in q["c1"]:
                c.wait_send()

    def gather_copies(buf, order=(0, 1)):
        g = {"own": [], "opp": [], "fwd": []}
        for s in order:
            g["own"].append(remote(buf.at[s, cr], buf.at[s, cr], sib))
            g["opp"].append([])
            for h in range(2):
                b = buf.at[s, cr, pl.ds(192 * h, 192)]
                g["opp"][-1].append(remote(b, b, opp))
            g["fwd"].append(remote(buf.at[s, oc], buf.at[s, oc], sib))
        return g

    def forward(g, s):
        for c in g["opp"][s]:
            c.wait_recv()
        g["fwd"][s].start()

    def send(g, s):
        for c in g["opp"][s]:
            c.start()
        g["own"][s].start()

    def arrived(g, s):
        g["own"][s].wait_recv()
        g["fwd"][s].wait_recv()

    def combine():
        cs = []
        for i, (half, dev) in enumerate(((1 - co, sib), (co, opp), (1 - co, ops))):
            c = remote(part.at[half], pin.at[i], dev)
            c.start()
            cs.append(c)
        return cs

    def solve_group(it, off):
        i = lax.rem(z + off, 8)
        x = rhs[it, i].reshape(768, 128)
        cols = pl.ds(pl.multiple_of(i * 768, 768), 768)
        return mm(km[:, cols], wide(x))

    def solve_most(it):
        def body(i, acc):
            return acc + solve_group(it, i + lax.div(i, 4))
        return lax.fori_loop(0, 7, body, jnp.zeros((96, 256), f32))

    def solve_rest(it, acc):
        co48[it, cr] = quad(acc + solve_group(it, 4), 48)
        cs = [remote(co48.at[it, cr], co48.at[it, cr], dev) for dev in (opp, ops, sib)]
        for c in cs:
            c.start()
        return cs

    def weights(it, s):
        first = co48[it, pl.ds(2 * s, 2)].reshape(96, 128)
        hi, lo = split(first)
        zero = jnp.zeros((32, 128), bf16)
        left = jnp.concatenate([hi, zero, hi, zero], axis=0)
        right = jnp.concatenate([lo, zero, jnp.zeros((128, 128), bf16)], axis=0)
        return jnp.concatenate([left, right], axis=1)

    def rebuild(it, s):
        w = weights(it, s)

        def body(j, carry):
            rows = pl.ds(pl.multiple_of(j * 384, 384), 384)
            v = lb[it, s, j] + halves(mm(bt[s, rows, :], w))
            xs[s, rows, :] = wide(v)
            return carry
        lax.fori_loop(0, 4, body, 0)
        rows = pl.ds(pl.multiple_of(cr * 384, 384), 384)
        v = lb[it, s, cr] + halves(mm(bt[s, rows, :], w))
        if it == 0:
            vsum[s] = v
        else:
            out[0, s] = vsum[s] + v

    def pick(m, s, g):
        return halves(mm(pickm[m, 384 * g:384 * (g + 1)], xs[s]))

    ld_b.wait()
    for s in range(2):
        hi, lo = split(bf[s, cr, 0:96, :])
        bo[s, 0:96] = hi
        bo[s, 96:192] = lo
    ld_r.wait()
    for s in range(2):
        part[s] = quad(mm(bo[s], wide(rb[0, s, cr])), 96)
    for c in ld_i:
        c.wait()
    wanted = [-1, -2, 2, 3, 1 - co]
    for k in range(6):
        near = nbr[co, k] - 2 * d
        on = (cnt[co] > k).astype(jnp.int32)
        row = read_rows[k, pl.ds(co, 1), :]
        for a in range(5):
            h = (near == wanted[a]).astype(jnp.int32) * on
            lists[a, k:k + 1, :] = row * h + (h - 1)

    @pl.when(co == 0)
    def _():
        pl.semaphore_wait(bar, 12)

    @pl.when(co == 1)
    def _():
        pl.semaphore_wait(bar, 11)

    c_part = combine()
    c_list_dn = remote(lists.at[pl.ds(0, 2)], rl.at[0], dn)
    c_list_up = remote(lists.at[pl.ds(2, 2)], rl.at[1], up)
    c_b1 = remote(bf.at[1 - cc, cr, pl.ds(0, 96)], bf.at[1 - cc, cr, pl.ds(0, 96)], otwin)
    c_b2 = remote(bf.at[cc, oc, pl.ds(0, 96)], bf.at[cc, oc, pl.ds(0, 96)], twin)
    c_bs = remote(bf.at[:, cr, pl.ds(0, 96)], bf.at[:, cr, pl.ds(0, 96)], sib)
    c_bo = remote(bf.at[:, oc, pl.ds(0, 96)], bf.at[:, oc, pl.ds(0, 96)], sib)
    c_b1.start()
    gr = gather_copies(rb.at[0])
    for s in range(2):
        send(gr, s)
    c_list_dn.start()
    c_list_up.start()
    c_bs.start()

    def zero_pad(j, carry):
        for s in range(2):
            bf[s, j, 96:128, :] = jnp.zeros((32, 384), f32)
        return carry
    lax.fori_loop(0, 4, zero_pad, 0)
    ld_l[0].wait()
    conv_matrix(0, 0)
    ld_s0 = load(6, s_hbm.at[0], stage.at[0])
    ld_l[1].wait()
    conv_matrix(0, 1)
    ld_s1 = load(7, s_hbm.at[1], stage.at[1])

    for c in c_part:
        c.wait_recv()
    rhs[0, z, y, co] = (part[co] + pin[0]) + (pin[1] + pin[2])
    q = coarse_copies(0)
    coarse_step(q, 0)
    ld_k.wait()
    hi, lo = split(kst[...])
    km[0:48] = hi
    km[48:96] = lo
    c_list_dn.wait_recv()
    c_list_up.wait_recv()
    build_pick(0, lambda k: rl[0, 0, pl.ds(k, 1), :])
    coarse_step(q, 1)
    build_pick(1, lambda k: rl[1, 0, pl.ds(k, 1), :])
    coarse_step(q, 2)
    forward(gr, 0)
    build_scatter(0)
    coarse_step(q, 3)
    gl = gather_copies(lb.at[0])
    arrived(gr, 0)
    for j in range(4):
        store_x(0, j, rb[0, 0, j])
    lb[0, 0, cr] = apply(0, 0)
    send(gl, 0)
    coarse_step(q, 4)
    c_b1.wait_recv()
    c_b2.start()
    build_pick(2, lambda k: rl[co, 1, pl.ds(k, 1), :])
    forward(gr, 1)
    coarse_step(q, 5)
    arrived(gr, 1)
    for j in range(4):
        store_x(1, j, rb[0, 1, j])
    lb[0, 1, cr] = apply(0, 1)
    gl["opp"][1][0].start()
    gl["own"][1].start()
    coarse_step(q, 7)
    acc = solve_most(0)
    coarse_step(q, 6)
    coarse_step(q, 8)
    cs = solve_rest(0, acc)
    gl["opp"][1][1].start()
    ld_s0.wait()
    conv_matrix(1, 0)
    ld_s1.wait()
    conv_matrix(1, 1)
    build_pick(3, lambda k: lists[4, pl.ds(k, 1), :])
    forward(gl, 0)
    c_b2.wait_recv()
    c_bo.start()
    build_scatter(1)
    c_bs.wait_recv()
    c_bo.wait_recv()
    lax.fori_loop(0, 4, lambda j, carry: (build_bt(j), carry)[1], 0)
    for j in range(4):
        hi, lo = split(bf[co, j, 0:96, :])
        bw[0:96, 384 * j:384 * (j + 1)] = hi
        bw[96:192, 384 * j:384 * (j + 1)] = lo
    ld_c.wait()
    for k in range(6):
        hi, lo = split(cst[k])
        cm[k, 0:128] = hi
        cm[k, 128:256] = lo

    for it in range(ITERS):
        c_up = []
        c_dn = []
        for g in range(2):
            part_rows = pl.ds(384 * g, 384)
            c_up.append(remote(ps.at[it, 0, part_rows], fr.at[it, 0, part_rows], up))
            c_dn.append(remote(ps.at[it, 1, part_rows], fr.at[it, 1, part_rows], dn))
        if it == 1:
            arrived(gl, 0)
            arrived(gl, 1)
            for s in range(2):
                for j in range(4):
                    store_x(s, j, lb[1, s, j])
            for g in range(2):
                rows = slice(384 * g, 384 * (g + 1))
                ps[1, 1, rows] = pick(1, 0, g)
                ps[1, 0, rows] = pick(0, 1, g)
                ps[1, co, rows] = ps[1, co, rows] + pick(2, co, g)
            for c in cs:
                c.wait_recv()
            ws = [weights(1, 1), weights(1, 0), weights(1, co)]
            for g in range(2):
                rows = slice(384 * g, 384 * (g + 1))
                for m, dest in ((0, 0), (1, 1), (2, co)):
                    ps[1, dest, rows] = ps[1, dest, rows] + halves(mm(qm[m, rows], ws[m]))
                c_up[g].start()
                c_dn[g].start()
            rebuild(1, 0)
            rebuild(1, 1)
        if it == 0:
            for c in cs:
                c.wait_recv()
            arrived(gl, 0)
            rebuild(0, 0)
            forward(gl, 1)
            for g in range(2):
                rows = slice(384 * g, 384 * (g + 1))
                ps[0, 1, rows] = pick(1, 0, g)

                @pl.when(co == 0)
                def _():
                    c_dn[g].start()
            arrived(gl, 1)
            rebuild(0, 1)
            gy = gather_copies(rb.at[1])
            for g in range(2):
                rows = slice(384 * g, 384 * (g + 1))
                ps[0, 0, rows] = pick(0, 1, g)

                @pl.when(co == 1)
                def _():
                    c_up[g].start()
                ps[0, co, rows] = ps[0, co, rows] + pick(2, co, g)

                @pl.when(co == 0)
                def _():
                    c_up[g].start()

                @pl.when(co == 1)
                def _():
                    c_dn[g].start()
                rb[1, g, cr] = rb[0, g, cr] - damping * apply(1, g)
                send(gy, g)
        if it == 1:
            for s in range(2):
                res[s] = r1[s] - damping * apply(1, s)
        own_rows = [pick(3, 1 - co, g) for g in range(2)]
        c_tm = []
        for g in range(2):
            if it == 0:
                for m, src_s in ((0, 1), (1, 0)) if g == 0 else ((2, co),):
                    for h in range(2):
                        rows = slice(384 * h, 384 * (h + 1))
                        qm[m, rows] = mm(pickm[m, rows], bt[src_s]).astype(bf16)
            c_up[g].wait_recv()
            c_dn[g].wait_recv()
            part_rows = pl.ds(384 * g, 384)
            src = own_rows[g] + fr[it, 0, part_rows] + fr[it, 1, part_rows]
            for k in range(3):
                rows = slice(384 * g + 128 * k, 384 * g + 128 * (k + 1))
                tm[it, co, rows, :] = quad(
                    mm(cm[3 * g + k], wide(src[128 * k:128 * (k + 1)])), 128
                )
            c = remote(tm.at[it, co, part_rows], tm.at[it, co, part_rows], sib)
            c.start()
            c_tm.append(c)
            if it == 0:
                forward(gy, g)
        for c in c_tm:
            c.wait_recv()
        tx = [wide(tm[it, s]) for s in range(2)]
        own = pl.ds(pl.multiple_of(cr * 384, 384), 384)
        for s in range(2):
            own_inflow = halves(mm(tt[s, own, :], tx[s]))
            if it == 0:
                r1[s] = rb[1, s, cr] + damping * own_inflow
                store_x(s, cr, r1[s])
            else:
                out[1, s] = 0.5 * (res[s] + damping * own_inflow)
        if it == 0:
            coarse_drain(q)
            gl = gather_copies(lb.at[1], (co, 1 - co))

            def fill(s):
                def body(i, carry):
                    j = lax.rem(cr + i, 4)
                    rows = pl.ds(pl.multiple_of(j * 384, 384), 384)
                    v = rb[1, s, j] + damping * halves(mm(tt[s, rows, :], wide(tm[0, s])))
                    xs[s, rows, :] = wide(v)
                    return carry
                lax.fori_loop(1, 4, body, 0)

            arrived(gy, 0)
            arrived(gy, 1)
            fill(co)
            rhs[1, z, y, co] = quad(mm(bw[...], xs[co]), 96)
            q = coarse_copies(1)
            coarse_step(q, 0)
            lb[1, co, cr] = apply(0, co)
            send(gl, 0)
            fill(1 - co)
            coarse_step(q, 1)
            lb[1, 1 - co, cr] = apply(0, 1 - co)
            send(gl, 1)
            coarse_step(q, 2)
            for n in range(3, 6):
                coarse_step(q, n)
            forward(gl, 0)
            coarse_step(q, 7)
            acc = solve_most(1)
            coarse_step(q, 6)
            forward(gl, 1)
            coarse_step(q, 8)
            cs = solve_rest(1, acc)
    coarse_drain(q)
    for c in pending:
        c.wait_send()


N_COPIES = 260


def per_device(
    load_cases,
    stiffness,
    local_inverse,
    coarse_basis,
    coarse_inverse,
    coupling,
    target_local_rows,
    neighbour_read_rows,
    neighbour,
    counts,
):
    any_spec = pl.BlockSpec(memory_space=pl.ANY)
    vmem = pl.BlockSpec(memory_space=pltpu.VMEM)
    V = pltpu.VMEM
    both = pl.pallas_call(
        kernel,
        name="schwarz",
        out_shape=jax.ShapeDtypeStruct((2, 2, 384, 128), f32),
        in_specs=[any_spec] * 10,
        out_specs=vmem,
        scratch_shapes=[
            V((2, 2, 4, 384, 128), f32),
            V((2, 2, 4, 384, 128), f32),
            V((2, 4, 128, 384), f32),
            V((2, 1536, 256), bf16),
            V((2, 192, 384), bf16),
            V((192, 1536), bf16),
            V((2, 2, 768, 1536), bf16),
            V((2, 384, 1536), f32),
            V((48, 6144), f32),
            V((96, 6144), bf16),
            V((2, 8, 4, 2, 96, 128), f32),
            V((2, 1536, 256), bf16),
            V((2, 384, 128), f32),
            V((2, 96, 128), f32),
            V((3, 96, 128), f32),
            V((4, 768, 1536), bf16),
            V((3, 768, 256), bf16),
            V((2, 1536, 768), bf16),
            V((2, 2, 768, 128), f32),
            V((2, 2, 768, 128), f32),
            V((2, 2, 768, 128), f32),
            V((6, 128, 128), f32),
            V((6, 256, 128), bf16),
            V((2, 2, 8, 128), jnp.int32),
            V((2, 4, 48, 128), f32),
            V((2, 384, 128), f32),
            V((2, 384, 128), f32),
            V((6, 2, 128), jnp.int32),
            V((6, 2, 128), jnp.int32),
            pltpu.SMEM((2, 6), jnp.int32),
            pltpu.SMEM((2,), jnp.int32),
            V((5, 8, 128), jnp.int32),
            pltpu.SemaphoreType.DMA((12,)),
            pltpu.SemaphoreType.DMA((N_COPIES,)),
            pltpu.SemaphoreType.DMA((N_COPIES,)),
        ],
        compiler_params=pltpu.CompilerParams(
            collective_id=0, has_side_effects=True, vmem_limit_bytes=66_000_000
        ),
    )(
        load_cases, stiffness, local_inverse, coarse_basis, coarse_inverse, coupling,
        target_local_rows.transpose(1, 0, 2), neighbour_read_rows.transpose(1, 0, 2),
        neighbour, counts,
    )
    return damping * both[0], 2.0 * both[1]


def solution(mesh):
    finer = Mesh(
        mesh.devices.reshape(8, 4, mesh.shape["crow"], mesh.shape["ccol"]),
        ("sub_0", "sub_1", "crow", "ccol"),
    )
    placed = (
        P(SUB, "crow", "ccol"),
        P(SUB, "crow", None),
        P(SUB, "crow", None),
        P(SUB, None, "crow"),
        P(SUB_CROW, None),
        P(SUB, None, None, None),
        P(SUB, None, None),
        P(SUB, None, None),
        P(SUB, None),
        P(SUB),
    )
    return jax.shard_map(
        per_device,
        mesh=finer,
        in_specs=placed,
        out_specs=(P(SUB, "crow", "ccol"), P(SUB, "crow", "ccol")),
        check_vma=False,
    )
```

```python
import jax
import jax.numpy as jnp
from jax import lax
from jax.experimental import pallas as pl
from jax.experimental.pallas import tpu as pltpu
from jax.sharding import Mesh
from jax.sharding import PartitionSpec as P

ITERS = 2
SUB = ("sub_0", "sub_1")
SUB_CROW = ("sub_0", "sub_1", "crow")
AXES = ("sub_0", "sub_1", "crow", "ccol")

damping = 0.7
f32 = jnp.float32
bf16 = jnp.bfloat16


def split(x):
    hi = x.astype(bf16)
    lo = (x - hi.astype(f32)).astype(bf16)
    return hi, lo


def wide(x):
    hi, lo = split(x)
    return jnp.concatenate([hi, lo], axis=1)


def mm(a, b):
    return jnp.dot(a, b, preferred_element_type=f32)


def quad(acc, rows):
    return acc[:rows, :128] + acc[:rows, 128:] + acc[rows:, :128]


def halves(acc):
    return acc[:, :128] + acc[:, 128:]


def kernel(
    r_hbm, s_hbm, l_hbm, b_hbm, k_hbm, c_hbm, t_hbm, rows_hbm, nbr_hbm, cnt_hbm,
    out,
    rb, lb, bf, bt, bo, bw, am, stage, kst, km, rhs, xs, r1, part, pin,
    pickm, qm, tt, ps, fr, tm, cst, cm, rl, co48, vsum, res,
    targets, read_rows, nbr, cnt, lists,
    ldsem, ss, rs,
):
    z, y, cr, cc = [lax.axis_index(a) for a in AXES]
    co = lax.rem(cr, 2)
    oc = lax.rem(cr + 2, 4)
    sc = cr + 1 - 2 * co
    osc = lax.rem(sc + 2, 4)
    d = z * 4 + y
    d_up = lax.rem(d + 1, 32)
    d_dn = lax.rem(d + 31, 32)
    sib = (z, y, sc, cc)
    opp = (z, y, oc, cc)
    ops = (z, y, osc, cc)
    twin = (z, y, cr, 1 - cc)
    otwin = (z, y, oc, 1 - cc)
    up = (lax.div(d_up, 4), lax.rem(d_up, 4), cr, cc)
    dn = (lax.div(d_dn, 4), lax.rem(d_dn, 4), cr, cc)

    def yat(k):
        return (z, lax.rem(y + k, 4), cr, cc)

    def zat(k):
        return (lax.rem(z + k, 8), y, cr, cc)

    n_send = [0]
    n_recv = [0]
    tail = []

    def slot(count):
        i = count[0]
        count[0] += 1
        return i

    def remote(src, dst, dev, si, ri):
        return pltpu.make_async_remote_copy(
            src_ref=src, dst_ref=dst, send_sem=ss.at[si], recv_sem=rs.at[ri],
            device_id=dev, device_id_type=pl.DeviceIdType.MESH,
        )

    def take_recv(ref, ri):
        remote(ref, ref, sib, 0, ri).wait_recv()

    def take_send(ref, si):
        remote(ref, ref, sib, si, 0).wait_send()

    def send_slot(ref):
        i = slot(n_send)
        tail.append((ref, i))
        return i

    def load(i, src, dst):
        c = pltpu.make_async_copy(src, dst, ldsem.at[i])
        c.start()
        return c

    ld_b = load(0, b_hbm, bf.at[:, cr, pl.ds(0, 96)])
    ld_r = load(1, r_hbm, rb.at[0, :, cr])
    ld_i = [
        load(8, t_hbm, targets),
        load(9, rows_hbm, read_rows),
        load(10, nbr_hbm, nbr),
        load(11, cnt_hbm, cnt),
    ]
    ld_l = [load(2 + s, l_hbm.at[s], stage.at[s]) for s in range(2)]
    ld_k = load(4, k_hbm, kst)
    ld_c = load(5, c_hbm.at[co], cst)

    bar = pltpu.get_barrier_semaphore()

    def greet(devs):
        for dev in devs:
            pl.semaphore_signal(bar, inc=1, device_id=dev, device_id_type=pl.DeviceIdType.MESH)

    greet([sib, opp, ops, twin, otwin, up, dn])

    @pl.when(co == 0)
    def _():
        greet([yat(1), yat(2), yat(3), zat(1), zat(7)])

    @pl.when(co == 1)
    def _():
        greet([zat(1), zat(7), yat(1), yat(3)])

    def conv_matrix(m, s):
        def body(i, carry):
            rows = pl.ds(pl.multiple_of(i * 32, 32), 32)
            rows2 = pl.ds(pl.multiple_of(384 + i * 32, 32), 32)
            hi, lo = split(stage[s, rows, :])
            am[m, s, rows, :] = hi
            am[m, s, rows2, :] = lo
            return carry
        lax.fori_loop(0, 12, body, 0)

    lane = lax.broadcasted_iota(jnp.int32, (128, 128), 1)
    sub_iota = lax.broadcasted_iota(jnp.int32, (128, 128), 0)

    def build_pick(m, row_of):
        def body(k, carry):
            row = jnp.broadcast_to(row_of(k), (128, 128))
            col = jnp.transpose(row)
            rows = pl.ds(pl.multiple_of(k * 128, 128), 128)
            for t in range(12):
                pickm[m, rows, 128 * t:128 * (t + 1)] = jnp.where(
                    col == lane + 128 * t, 1.0, 0.0
                ).astype(bf16)
            return carry
        lax.fori_loop(0, 6, body, 0)

    def build_scatter(s):
        for k in range(6):
            row = jnp.broadcast_to(targets[k, s:s + 1, :], (128, 128))

            def body(t, carry):
                rows = pl.ds(pl.multiple_of(t * 128, 128), 128)
                tt[s, rows, 128 * k:128 * (k + 1)] = jnp.where(
                    row == sub_iota + 128 * t, 1.0, 0.0
                ).astype(bf16)
                return carry
            lax.fori_loop(0, 12, body, 0)

    def build_bt(j):
        for s in range(2):
            t = jnp.transpose(bf[s, j])
            rows = pl.ds(pl.multiple_of(j * 384, 384), 384)
            bt[s, rows, :] = wide(t)

    def store_x(s, j, value):
        rows = pl.ds(pl.multiple_of(j * 384, 384), 384)
        xs[s, rows, :] = wide(value)

    def apply(m, s):
        return quad(mm(am[m, s], xs[s]), 384)

    def coarse_copies(it):
        q = {}
        g = rhs.at[it]
        first = n_recv[0]
        links = [slot(n_send), slot(n_send)]
        chip = send_slot(g.at[pl.ds(0, 4)])

        def block(zz, yy, half, dev, si, ri):
            b = g.at[zz, yy, half]
            return remote(b, b, dev, si, ri)

        def link(zz, yy, half, dev, way):
            return block(zz, yy, half, dev, links[way], slot(n_recv))

        def zm(k):
            return lax.rem(z + 8 + k, 8)

        def ym(k):
            return lax.rem(y + 4 + k, 4)

        for k in (1, 3, 2):
            q["y", k] = link(z, y, 0, yat(k), 0)
        for j in range(4):
            for h in range(1, 5):
                if h < 4 or j < 2:
                    q["p", j, h] = link(zm(1 - h), ym(-j), 0, zat(1), 1)
                if h < 4 or j >= 2:
                    q["m", j, h] = link(zm(h - 1), ym(-j), 0, zat(7), 1)
        keys0 = list(q)
        last = n_recv[0]
        n_recv[0] = first
        for h in range(1, 5):
            q["s", h] = link(zm(1 - h), y, 1, zat(1), 0)
            if h < 4:
                q["t", h] = link(zm(h - 1), y, 1, zat(7), 0)
        for k in range(8):
            for h in range(1, 3):
                if h < 2 or k % 2 == 0:
                    q["u", k, h] = link(zm(-k), ym(1 - h), 1, yat(1), 1)
                if h < 2 or k % 2 == 1:
                    q["v", k, h] = link(zm(-k), ym(h - 1), 1, yat(3), 1)
        keys1 = [k for k in q if k not in keys0]
        n_recv[0] = max(last, n_recv[0])
        chips = [slot(n_recv), slot(n_recv)]
        f0 = {}
        def chip0(key, zz, yy):
            f0[key] = block(zz, yy, 0, sib, chip, chips[key[-1] == 4])

        def chip1(key, zz, yy):
            f1[key] = block(zz, yy, 1, sib, chip, chips[key[1] == 4])

        for k in range(4):
            chip0(("y", k), z, ym(-k))
        for key in keys0:
            if key[0] == "p":
                chip0(key, zm(-key[2]), ym(-key[1]))
            if key[0] == "m":
                chip0(key, zm(key[2]), ym(-key[1]))
        f1 = {}
        for k in range(8):
            chip1(("z", k), zm(-k), y)
        for key in keys1:
            if key[0] == "u":
                chip1(key, zm(-key[1]), ym(-key[2]))
            if key[0] == "v":
                chip1(key, zm(-key[1]), ym(key[2]))
        assert len(f0) == len(f1) == 32
        q["f0"] = f0
        q["f1"] = f1
        q["links"] = links
        q["chips"] = chips
        q["g"] = g
        return q

    def coarse_step(q, n):
        def relay(f, a, b, j, hops):
            for h in hops:
                for way in (a, b):
                    if (way, j, h) in q:
                        q[way, j, h].wait_recv()
                        if (way, j, h + 1) in q:
                            q[way, j, h + 1].start()
                        f[way, j, h].start()

        @pl.when(co == 0)
        def _():
            f = q["f0"]

            def enter(k):
                q["y", k].wait_recv()
                q["p", k, 1].start()
                q["m", k, 1].start()
                f["y", k].start()

            if n == 0:
                for k in (1, 3, 2):
                    q["y", k].start()
                q["p", 0, 1].start()
                q["m", 0, 1].start()
                f["y", 0].start()
            if n == 1:
                relay(f, "p", "m", 0, [1])
                enter(1)
                enter(3)
            if n == 2:
                enter(2)
                relay(f, "p", "m", 0, [2])
            if 3 <= n <= 6:
                for j in (1, 3, 2):
                    relay(f, "p", "m", j, [n - 2])
                if n < 5:
                    relay(f, "p", "m", 0, [n])

        @pl.when(co == 1)
        def _():
            f = q["f1"]

            def enter(h):
                for way, k in (("s", h), ("t", 8 - h)):
                    if (way, h) in q:
                        q[way, h].wait_recv()
                        if (way, h + 1) in q:
                            q[way, h + 1].start()
                        q["u", k, 1].start()
                        q["v", k, 1].start()
                        f["z", k].start()

            def both(h, hop):
                for k in sorted({h % 8, (8 - h) % 8}):
                    relay(f, "u", "v", k, [hop])

            if n == 0:
                q["s", 1].start()
                q["t", 1].start()
                q["u", 0, 1].start()
                q["v", 0, 1].start()
                f["z", 0].start()
            if 1 <= n <= 4:
                enter(n)
            if 1 <= n <= 5:
                both(n - 1, 1)
            if 2 <= n <= 6:
                both(n - 2, 2)

        if n == 7:
            take_recv(q["g"].at[pl.ds(0, 7), :, 0], q["chips"][0])
        if n == 8:
            take_recv(q["g"].at[0, :, 0], q["chips"][1])

    def coarse_drain(q):
        g = q["g"]

        @pl.when(co == 0)
        def _():
            take_send(g.at[0, pl.ds(0, 3), 0], q["links"][0])
            take_send(g.at[pl.ds(0, 7), :, 0], q["links"][1])

        @pl.when(co == 1)
        def _():
            take_send(g.at[pl.ds(0, 7), 0, 0], q["links"][0])
            take_send(g.at[pl.ds(0, 3)], q["links"][1])

    def gather_copies(buf, order=(0, 1)):
        g = {"own": [], "opp": [], "fwd": [], "near": [], "far": [], "buf": buf}
        si = send_slot(buf.at[:, pl.ds(0, 3)])
        for s in order:
            near = slot(n_recv)
            far = slot(n_recv)
            g["near"].append(near)
            g["far"].append(far)
            g["own"].append(remote(buf.at[s, cr], buf.at[s, cr], sib, si, near))
            g["opp"].append([])
            for h in range(2):
                b = buf.at[s, cr, pl.ds(192 * h, 192)]
                g["opp"][-1].append(remote(b, b, opp, si, far))
            g["fwd"].append(remote(buf.at[s, oc], buf.at[s, oc], sib, si, near))
        return g

    def forward(g, s):
        take_recv(g["buf"].at[0, 0], g["far"][s])
        g["fwd"][s].start()

    def send(g, s):
        for c in g["opp"][s]:
            c.start()
        g["own"][s].start()

    def arrived(g, s):
        take_recv(g["buf"].at[0, pl.ds(0, 2)], g["near"][s])

    def combine():
        si = send_slot(pin)
        ri = slot(n_recv)
        for i, (half, dev) in enumerate(((1 - co, sib), (co, opp), (1 - co, ops))):
            remote(part.at[half], pin.at[i], dev, si, ri).start()
        return ri

    def solve_group(it, off):
        i = lax.rem(z + off, 8)
        x = rhs[it, i].reshape(768, 128)
        cols = pl.ds(pl.multiple_of(i * 768, 768), 768)
        return mm(km[:, cols], wide(x))

    def solve_most(it):
        def body(i, acc):
            return acc + solve_group(it, i + lax.div(i, 4))
        return lax.fori_loop(0, 7, body, jnp.zeros((96, 256), f32))

    def solve_rest(it, acc):
        co48[it, cr] = quad(acc + solve_group(it, 4), 48)
        si = send_slot(co48.at[it, pl.ds(0, 3)])
        ri = slot(n_recv)
        for dev in (opp, ops, sib):
            remote(co48.at[it, cr], co48.at[it, cr], dev, si, ri).start()
        return ri

    def weights(it, s):
        first = co48[it, pl.ds(2 * s, 2)].reshape(96, 128)
        hi, lo = split(first)
        zero = jnp.zeros((32, 128), bf16)
        left = jnp.concatenate([hi, zero, hi, zero], axis=0)
        right = jnp.concatenate([lo, zero, jnp.zeros((128, 128), bf16)], axis=0)
        return jnp.concatenate([left, right], axis=1)

    def rebuild(it, s):
        w = weights(it, s)

        def body(j, carry):
            rows = pl.ds(pl.multiple_of(j * 384, 384), 384)
            v = lb[it, s, j] + halves(mm(bt[s, rows, :], w))
            xs[s, rows, :] = wide(v)
            return carry
        lax.fori_loop(0, 4, body, 0)
        rows = pl.ds(pl.multiple_of(cr * 384, 384), 384)
        v = lb[it, s, cr] + halves(mm(bt[s, rows, :], w))
        if it == 0:
            vsum[s] = v
        else:
            out[0, s] = vsum[s] + v

    def pick(m, s, g):
        return halves(mm(pickm[m, 384 * g:384 * (g + 1)], xs[s]))

    ld_b.wait()
    for s in range(2):
        hi, lo = split(bf[s, cr, 0:96, :])
        bo[s, 0:96] = hi
        bo[s, 96:192] = lo
    ld_r.wait()
    for s in range(2):
        part[s] = quad(mm(bo[s], wide(rb[0, s, cr])), 96)
    for c in ld_i:
        c.wait()
    wanted = [-1, -2, 2, 3, 1 - co]
    for k in range(6):
        near = nbr[co, k] - 2 * d
        on = (cnt[co] > k).astype(jnp.int32)
        row = read_rows[k, pl.ds(co, 1), :]
        for a in range(5):
            h = (near == wanted[a]).astype(jnp.int32) * on
            lists[a, k:k + 1, :] = row * h + (h - 1)

    @pl.when(co == 0)
    def _():
        pl.semaphore_wait(bar, 12)

    @pl.when(co == 1)
    def _():
        pl.semaphore_wait(bar, 11)

    c_part = combine()
    s_list = send_slot(rl)
    r_list = slot(n_recv)
    c_list_dn = remote(lists.at[pl.ds(0, 2)], rl.at[0], dn, s_list, r_list)
    c_list_up = remote(lists.at[pl.ds(2, 2)], rl.at[1], up, s_list, r_list)
    s_b = send_slot(bf.at[:, pl.ds(0, 3), pl.ds(0, 96)])
    r_b = [slot(n_recv) for _ in range(3)]

    def basis(at, dev, ri):
        b = bf.at[at + (pl.ds(0, 96),)]
        return remote(b, b, dev, s_b, r_b[ri])

    c_b1 = basis((1 - cc, cr), otwin, 0)
    c_b2 = basis((cc, oc), twin, 1)
    c_bs = basis((slice(None), cr), sib, 2)
    c_bo = basis((slice(None), oc), sib, 2)
    c_b1.start()
    gr = gather_copies(rb.at[0])
    for s in range(2):
        send(gr, s)
    c_list_dn.start()
    c_list_up.start()
    c_bs.start()

    def zero_pad(j, carry):
        for s in range(2):
            bf[s, j, 96:128, :] = jnp.zeros((32, 384), f32)
        return carry
    lax.fori_loop(0, 4, zero_pad, 0)
    ld_l[0].wait()
    conv_matrix(0, 0)
    ld_s0 = load(6, s_hbm.at[0], stage.at[0])
    ld_l[1].wait()
    conv_matrix(0, 1)
    ld_s1 = load(7, s_hbm.at[1], stage.at[1])

    take_recv(pin, c_part)
    rhs[0, z, y, co] = (part[co] + pin[0]) + (pin[1] + pin[2])
    q = coarse_copies(0)
    coarse_step(q, 0)
    ld_k.wait()
    hi, lo = split(kst[...])
    km[0:48] = hi
    km[48:96] = lo
    take_recv(rl, r_list)
    build_pick(0, lambda k: rl[0, 0, pl.ds(k, 1), :])
    coarse_step(q, 1)
    build_pick(1, lambda k: rl[1, 0, pl.ds(k, 1), :])
    coarse_step(q, 2)
    forward(gr, 0)
    build_scatter(0)
    coarse_step(q, 3)
    gl = gather_copies(lb.at[0])
    arrived(gr, 0)
    for j in range(4):
        store_x(0, j, rb[0, 0, j])
    lb[0, 0, cr] = apply(0, 0)
    send(gl, 0)
    coarse_step(q, 4)
    c_b1.wait_recv()
    c_b2.start()
    build_pick(2, lambda k: rl[co, 1, pl.ds(k, 1), :])
    forward(gr, 1)
    coarse_step(q, 5)
    arrived(gr, 1)
    for j in range(4):
        store_x(1, j, rb[0, 1, j])
    lb[0, 1, cr] = apply(0, 1)
    gl["opp"][1][0].start()
    gl["own"][1].start()
    coarse_step(q, 7)
    acc = solve_most(0)
    coarse_step(q, 6)
    coarse_step(q, 8)
    cs = solve_rest(0, acc)
    gl["opp"][1][1].start()
    ld_s0.wait()
    conv_matrix(1, 0)
    ld_s1.wait()
    conv_matrix(1, 1)
    build_pick(3, lambda k: lists[4, pl.ds(k, 1), :])
    forward(gl, 0)
    c_b2.wait_recv()
    c_bo.start()
    build_scatter(1)
    take_recv(bf.at[:, pl.ds(0, 2), pl.ds(0, 96)], r_b[2])
    lax.fori_loop(0, 4, lambda j, carry: (build_bt(j), carry)[1], 0)
    for j in range(4):
        hi, lo = split(bf[co, j, 0:96, :])
        bw[0:96, 384 * j:384 * (j + 1)] = hi
        bw[96:192, 384 * j:384 * (j + 1)] = lo
    ld_c.wait()
    for k in range(6):
        hi, lo = split(cst[k])
        cm[k, 0:128] = hi
        cm[k, 128:256] = lo

    for it in range(ITERS):
        c_up = []
        c_dn = []
        s_ps = send_slot(ps.at[it])
        r_fr = []
        for g in range(2):
            part_rows = pl.ds(384 * g, 384)
            r_fr.append(slot(n_recv))
            c_up.append(remote(ps.at[it, 0, part_rows], fr.at[it, 0, part_rows], up, s_ps, r_fr[g]))
            c_dn.append(remote(ps.at[it, 1, part_rows], fr.at[it, 1, part_rows], dn, s_ps, r_fr[g]))
        if it == 1:
            arrived(gl, 0)
            arrived(gl, 1)
            for s in range(2):
                for j in range(4):
                    store_x(s, j, lb[1, s, j])
            for g in range(2):
                rows = slice(384 * g, 384 * (g + 1))
                ps[1, 1, rows] = pick(1, 0, g)
                ps[1, 0, rows] = pick(0, 1, g)
                ps[1, co, rows] = ps[1, co, rows] + pick(2, co, g)
            take_recv(co48.at[it, pl.ds(0, 3)], cs)
            ws = [weights(1, 1), weights(1, 0), weights(1, co)]
            for g in range(2):
                rows = slice(384 * g, 384 * (g + 1))
                for m, dest in ((0, 0), (1, 1), (2, co)):
                    ps[1, dest, rows] = ps[1, dest, rows] + halves(mm(qm[m, rows], ws[m]))
                c_up[g].start()
                c_dn[g].start()
            rebuild(1, 0)
            rebuild(1, 1)
        if it == 0:
            take_recv(co48.at[it, pl.ds(0, 3)], cs)
            arrived(gl, 0)
            rebuild(0, 0)
            forward(gl, 1)
            for g in range(2):
                rows = slice(384 * g, 384 * (g + 1))
                ps[0, 1, rows] = pick(1, 0, g)

                @pl.when(co == 0)
                def _():
                    c_dn[g].start()
            arrived(gl, 1)
            rebuild(0, 1)
            gy = gather_copies(rb.at[1])
            for g in range(2):
                rows = slice(384 * g, 384 * (g + 1))
                ps[0, 0, rows] = pick(0, 1, g)

                @pl.when(co == 1)
                def _():
                    c_up[g].start()
                ps[0, co, rows] = ps[0, co, rows] + pick(2, co, g)

                @pl.when(co == 0)
                def _():
                    c_up[g].start()

                @pl.when(co == 1)
                def _():
                    c_dn[g].start()
                rb[1, g, cr] = rb[0, g, cr] - damping * apply(1, g)
                send(gy, g)
        if it == 1:
            for s in range(2):
                res[s] = r1[s] - damping * apply(1, s)
        own_rows = [pick(3, 1 - co, g) for g in range(2)]
        s_tm = send_slot(tm.at[it, 0])
        r_tm = slot(n_recv)
        for g in range(2):
            if it == 0:
                for m, src_s in ((0, 1), (1, 0)) if g == 0 else ((2, co),):
                    for h in range(2):
                        rows = slice(384 * h, 384 * (h + 1))
                        qm[m, rows] = mm(pickm[m, rows], bt[src_s]).astype(bf16)
            part_rows = pl.ds(384 * g, 384)
            take_recv(fr.at[it, :, part_rows], r_fr[g])
            src = own_rows[g] + fr[it, 0, part_rows] + fr[it, 1, part_rows]
            for k in range(3):
                rows = slice(384 * g + 128 * k, 384 * g + 128 * (k + 1))
                tm[it, co, rows, :] = quad(
                    mm(cm[3 * g + k], wide(src[128 * k:128 * (k + 1)])), 128
                )
            terms = tm.at[it, co, part_rows]
            remote(terms, terms, sib, s_tm, r_tm).start()
            if it == 0:
                forward(gy, g)
        take_recv(tm.at[it, 0], r_tm)
        tx = [wide(tm[it, s]) for s in range(2)]
        own = pl.ds(pl.multiple_of(cr * 384, 384), 384)
        for s in range(2):
            own_inflow = halves(mm(tt[s, own, :], tx[s]))
            if it == 0:
                r1[s] = rb[1, s, cr] + damping * own_inflow
                store_x(s, cr, r1[s])
            else:
                out[1, s] = 0.5 * (res[s] + damping * own_inflow)
        if it == 0:
            coarse_drain(q)
            gl = gather_copies(lb.at[1], (co, 1 - co))

            def fill(s):
                def body(i, carry):
                    j = lax.rem(cr + i, 4)
                    rows = pl.ds(pl.multiple_of(j * 384, 384), 384)
                    v = rb[1, s, j] + damping * halves(mm(tt[s, rows, :], wide(tm[0, s])))
                    xs[s, rows, :] = wide(v)
                    return carry
                lax.fori_loop(1, 4, body, 0)

            arrived(gy, 0)
            arrived(gy, 1)
            fill(co)
            rhs[1, z, y, co] = quad(mm(bw[...], xs[co]), 96)
            q = coarse_copies(1)
            coarse_step(q, 0)
            lb[1, co, cr] = apply(0, co)
            send(gl, 0)
            fill(1 - co)
            coarse_step(q, 1)
            lb[1, 1 - co, cr] = apply(0, 1 - co)
            send(gl, 1)
            coarse_step(q, 2)
            for n in range(3, 6):
                coarse_step(q, n)
            forward(gl, 0)
            coarse_step(q, 7)
            acc = solve_most(1)
            coarse_step(q, 6)
            forward(gl, 1)
            coarse_step(q, 8)
            cs = solve_rest(1, acc)
    coarse_drain(q)
    for ref, i in tail:
        take_send(ref, i)
    assert n_send[0] == N_SEND and n_recv[0] == N_RECV, (n_send, n_recv)


N_SEND = 19
N_RECV = 95


def per_device(
    load_cases,
    stiffness,
    local_inverse,
    coarse_basis,
    coarse_inverse,
    coupling,
    target_local_rows,
    neighbour_read_rows,
    neighbour,
    counts,
):
    any_spec = pl.BlockSpec(memory_space=pl.ANY)
    vmem = pl.BlockSpec(memory_space=pltpu.VMEM)
    V = pltpu.VMEM
    both = pl.pallas_call(
        kernel,
        name="schwarz",
        out_shape=jax.ShapeDtypeStruct((2, 2, 384, 128), f32),
        in_specs=[any_spec] * 10,
        out_specs=vmem,
        scratch_shapes=[
            V((2, 2, 4, 384, 128), f32),
            V((2, 2, 4, 384, 128), f32),
            V((2, 4, 128, 384), f32),
            V((2, 1536, 256), bf16),
            V((2, 192, 384), bf16),
            V((192, 1536), bf16),
            V((2, 2, 768, 1536), bf16),
            V((2, 384, 1536), f32),
            V((48, 6144), f32),
            V((96, 6144), bf16),
            V((2, 8, 4, 2, 96, 128), f32),
            V((2, 1536, 256), bf16),
            V((2, 384, 128), f32),
            V((2, 96, 128), f32),
            V((3, 96, 128), f32),
            V((4, 768, 1536), bf16),
            V((3, 768, 256), bf16),
            V((2, 1536, 768), bf16),
            V((2, 2, 768, 128), f32),
            V((2, 2, 768, 128), f32),
            V((2, 2, 768, 128), f32),
            V((6, 128, 128), f32),
            V((6, 256, 128), bf16),
            V((2, 2, 8, 128), jnp.int32),
            V((2, 4, 48, 128), f32),
            V((2, 384, 128), f32),
            V((2, 384, 128), f32),
            V((6, 2, 128), jnp.int32),
            V((6, 2, 128), jnp.int32),
            pltpu.SMEM((2, 6), jnp.int32),
            pltpu.SMEM((2,), jnp.int32),
            V((5, 8, 128), jnp.int32),
            pltpu.SemaphoreType.DMA((12,)),
            pltpu.SemaphoreType.DMA((N_SEND,)),
            pltpu.SemaphoreType.DMA((N_RECV,)),
        ],
        compiler_params=pltpu.CompilerParams(
            collective_id=0, has_side_effects=True, vmem_limit_bytes=66_000_000
        ),
    )(
        load_cases, stiffness, local_inverse, coarse_basis, coarse_inverse, coupling,
        target_local_rows.transpose(1, 0, 2), neighbour_read_rows.transpose(1, 0, 2),
        neighbour, counts,
    )
    return damping * both[0], 2.0 * both[1]


def solution(mesh):
    finer = Mesh(
        mesh.devices.reshape(8, 4, mesh.shape["crow"], mesh.shape["ccol"]),
        ("sub_0", "sub_1", "crow", "ccol"),
    )
    placed = (
        P(SUB, "crow", "ccol"),
        P(SUB, "crow", None),
        P(SUB, "crow", None),
        P(SUB, None, "crow"),
        P(SUB_CROW, None),
        P(SUB, None, None, None),
        P(SUB, None, None),
        P(SUB, None, None),
        P(SUB, None),
        P(SUB),
    )
    return jax.shard_map(
        per_device,
        mesh=finer,
        in_specs=placed,
        out_specs=(P(SUB, "crow", "ccol"), P(SUB, "crow", "ccol")),
        check_vma=False,
    )
```

```python
import jax
import jax.numpy as jnp
from jax import lax
from jax.experimental import pallas as pl
from jax.experimental.pallas import tpu as pltpu
from jax.sharding import Mesh
from jax.sharding import PartitionSpec as P

ITERS = 2
SUB = ("sub_0", "sub_1")
SUB_CROW = ("sub_0", "sub_1", "crow")
AXES = ("sub_0", "sub_1", "crow", "ccol")

damping = 0.7
f32 = jnp.float32
bf16 = jnp.bfloat16


def split(x):
    hi = x.astype(bf16)
    lo = (x - hi.astype(f32)).astype(bf16)
    return hi, lo


def wide(x):
    hi, lo = split(x)
    return jnp.concatenate([hi, lo], axis=1)


def mm(a, b):
    return jnp.dot(a, b, preferred_element_type=f32)


def quad(acc, rows):
    return acc[:rows, :128] + acc[:rows, 128:] + acc[rows:, :128]


def halves(acc):
    return acc[:, :128] + acc[:, 128:]


def kernel(
    r_hbm, s_hbm, l_hbm, b_hbm, k_hbm, c_hbm, t_hbm, rows_hbm, nbr_hbm, cnt_hbm,
    out,
    rb, lb, bf, bt, bo, bw, am, stage, kst, km, rhs, xs, r1, part, pin,
    pickm, qm, tt, ps, fr, tm, cst, cm, rl, co48, vsum, res,
    targets, read_rows, nbr, cnt, lists,
    ldsem, ss, rs,
):
    z, y, cr, cc = [lax.axis_index(a) for a in AXES]
    co = lax.rem(cr, 2)
    oc = lax.rem(cr + 2, 4)
    sc = cr + 1 - 2 * co
    osc = lax.rem(sc + 2, 4)
    d = z * 4 + y
    d_up = lax.rem(d + 1, 32)
    d_dn = lax.rem(d + 31, 32)
    sib = (z, y, sc, cc)
    opp = (z, y, oc, cc)
    ops = (z, y, osc, cc)
    twin = (z, y, cr, 1 - cc)
    otwin = (z, y, oc, 1 - cc)
    up = (lax.div(d_up, 4), lax.rem(d_up, 4), cr, cc)
    dn = (lax.div(d_dn, 4), lax.rem(d_dn, 4), cr, cc)

    def yat(k):
        return (z, lax.rem(y + k, 4), cr, cc)

    def zat(k):
        return (lax.rem(z + k, 8), y, cr, cc)

    n_send = [0]
    n_recv = [0]
    tail = []

    def slot(count):
        i = count[0]
        count[0] += 1
        return i

    def remote(src, dst, dev, si, ri):
        return pltpu.make_async_remote_copy(
            src_ref=src, dst_ref=dst, send_sem=ss.at[si], recv_sem=rs.at[ri],
            device_id=dev, device_id_type=pl.DeviceIdType.MESH,
        )

    def take_recv(ref, ri):
        remote(ref, ref, sib, 0, ri).wait_recv()

    def take_send(ref, si):
        remote(ref, ref, sib, si, 0).wait_send()

    def send_slot(ref):
        i = slot(n_send)
        tail.append((ref, i))
        return i

    def load(i, src, dst):
        c = pltpu.make_async_copy(src, dst, ldsem.at[i])
        c.start()
        return c

    ld_b = load(0, b_hbm, bf.at[:, cr, pl.ds(0, 96)])
    ld_r = load(1, r_hbm, rb.at[0, :, cr])
    ld_i = [
        load(8, t_hbm, targets),
        load(9, rows_hbm, read_rows),
        load(10, nbr_hbm, nbr),
        load(11, cnt_hbm, cnt),
    ]
    ld_l = [load(2 + s, l_hbm.at[s], stage.at[s]) for s in range(2)]
    ld_k = load(4, k_hbm, kst)
    ld_c = load(5, c_hbm.at[co], cst)

    bar = pltpu.get_barrier_semaphore()

    def greet(devs):
        for dev in devs:
            pl.semaphore_signal(bar, inc=1, device_id=dev, device_id_type=pl.DeviceIdType.MESH)

    greet([sib, opp, ops, twin, otwin, up, dn])

    @pl.when(co == 0)
    def _():
        greet([yat(1), yat(2), yat(3), zat(1), zat(7)])

    @pl.when(co == 1)
    def _():
        greet([zat(1), zat(7), yat(1), yat(3)])

    def conv_matrix(m, s):
        def body(i, carry):
            rows = pl.ds(pl.multiple_of(i * 32, 32), 32)
            rows2 = pl.ds(pl.multiple_of(384 + i * 32, 32), 32)
            hi, lo = split(stage[s, rows, :])
            am[m, s, rows, :] = hi
            am[m, s, rows2, :] = lo
            return carry
        lax.fori_loop(0, 12, body, 0)

    lane = lax.broadcasted_iota(jnp.int32, (128, 128), 1)
    sub_iota = lax.broadcasted_iota(jnp.int32, (128, 128), 0)

    def build_pick(m, row_of):
        def body(k, carry):
            row = jnp.broadcast_to(row_of(k), (128, 128))
            col = jnp.transpose(row)
            rows = pl.ds(pl.multiple_of(k * 128, 128), 128)
            for t in range(12):
                pickm[m, rows, 128 * t:128 * (t + 1)] = jnp.where(
                    col == lane + 128 * t, 1.0, 0.0
                ).astype(bf16)
            return carry
        lax.fori_loop(0, 6, body, 0)

    def build_scatter(s):
        for k in range(6):
            row = jnp.broadcast_to(targets[k, s:s + 1, :], (128, 128))

            def body(t, carry):
                rows = pl.ds(pl.multiple_of(t * 128, 128), 128)
                tt[s, rows, 128 * k:128 * (k + 1)] = jnp.where(
                    row == sub_iota + 128 * t, 1.0, 0.0
                ).astype(bf16)
                return carry
            lax.fori_loop(0, 12, body, 0)

    def build_bt(j):
        for s in range(2):
            t = jnp.transpose(bf[s, j])
            rows = pl.ds(pl.multiple_of(j * 384, 384), 384)
            bt[s, rows, :] = wide(t)

    def store_x(s, j, value):
        rows = pl.ds(pl.multiple_of(j * 384, 384), 384)
        xs[s, rows, :] = wide(value)

    def apply(m, s):
        return quad(mm(am[m, s], xs[s]), 384)

    def coarse_copies(it):
        q = {}
        g = rhs.at[it]
        first = n_recv[0]
        links = [slot(n_send), slot(n_send)]
        chip = send_slot(g.at[pl.ds(0, 4)])

        def block(zz, yy, half, dev, si, ri):
            b = g.at[zz, yy, half]
            return remote(b, b, dev, si, ri)

        def link(zz, yy, half, dev, way):
            return block(zz, yy, half, dev, links[way], slot(n_recv))

        def zm(k):
            return lax.rem(z + 8 + k, 8)

        def ym(k):
            return lax.rem(y + 4 + k, 4)

        for k in (1, 3, 2):
            q["y", k] = link(z, y, 0, yat(k), 0)
        for j in range(4):
            for h in range(1, 5):
                if h < 4 or j < 2:
                    q["p", j, h] = link(zm(1 - h), ym(-j), 0, zat(1), 1)
                if h < 4 or j >= 2:
                    q["m", j, h] = link(zm(h - 1), ym(-j), 0, zat(7), 1)
        keys0 = list(q)
        last = n_recv[0]
        n_recv[0] = first
        for h in range(1, 5):
            q["s", h] = link(zm(1 - h), y, 1, zat(1), 0)
            if h < 4:
                q["t", h] = link(zm(h - 1), y, 1, zat(7), 0)
        for k in range(8):
            for h in range(1, 3):
                if h < 2 or k % 2 == 0:
                    q["u", k, h] = link(zm(-k), ym(1 - h), 1, yat(1), 1)
                if h < 2 or k % 2 == 1:
                    q["v", k, h] = link(zm(-k), ym(h - 1), 1, yat(3), 1)
        keys1 = [k for k in q if k not in keys0]
        n_recv[0] = max(last, n_recv[0])
        chips = [slot(n_recv), slot(n_recv)]
        f0 = {}
        def chip0(key, zz, yy):
            f0[key] = block(zz, yy, 0, sib, chip, chips[key[-1] == 4])

        def chip1(key, zz, yy):
            f1[key] = block(zz, yy, 1, sib, chip, chips[key[1] == 4])

        for k in range(4):
            chip0(("y", k), z, ym(-k))
        for key in keys0:
            if key[0] == "p":
                chip0(key, zm(-key[2]), ym(-key[1]))
            if key[0] == "m":
                chip0(key, zm(key[2]), ym(-key[1]))
        f1 = {}
        for k in range(8):
            chip1(("z", k), zm(-k), y)
        for key in keys1:
            if key[0] == "u":
                chip1(key, zm(-key[1]), ym(-key[2]))
            if key[0] == "v":
                chip1(key, zm(-key[1]), ym(key[2]))
        assert len(f0) == len(f1) == 32
        q["f0"] = f0
        q["f1"] = f1
        q["links"] = links
        q["chips"] = chips
        q["g"] = g
        return q

    def coarse_step(q, n):
        def relay(f, a, b, j, hops):
            for h in hops:
                for way in (a, b):
                    if (way, j, h) in q:
                        q[way, j, h].wait_recv()
                        if (way, j, h + 1) in q:
                            q[way, j, h + 1].start()
                        f[way, j, h].start()

        @pl.when(co == 0)
        def _():
            f = q["f0"]

            def enter(k):
                q["y", k].wait_recv()
                q["p", k, 1].start()
                q["m", k, 1].start()
                f["y", k].start()

            if n == 0:
                for k in (1, 3, 2):
                    q["y", k].start()
                q["p", 0, 1].start()
                q["m", 0, 1].start()
                f["y", 0].start()
            if n == 1:
                relay(f, "p", "m", 0, [1])
                enter(1)
                enter(3)
            if n == 2:
                enter(2)
                relay(f, "p", "m", 0, [2])
            if 3 <= n <= 6:
                for j in (1, 3, 2):
                    relay(f, "p", "m", j, [n - 2])
                if n < 5:
                    relay(f, "p", "m", 0, [n])

        @pl.when(co == 1)
        def _():
            f = q["f1"]

            def enter(h):
                for way, k in (("s", h), ("t", 8 - h)):
                    if (way, h) in q:
                        q[way, h].wait_recv()
                        if (way, h + 1) in q:
                            q[way, h + 1].start()
                        q["u", k, 1].start()
                        q["v", k, 1].start()
                        f["z", k].start()

            def both(h, hop):
                for k in sorted({h % 8, (8 - h) % 8}):
                    relay(f, "u", "v", k, [hop])

            if n == 0:
                q["s", 1].start()
                q["t", 1].start()
                q["u", 0, 1].start()
                q["v", 0, 1].start()
                f["z", 0].start()
            if 1 <= n <= 4:
                enter(n)
            if 1 <= n <= 5:
                both(n - 1, 1)
            if 2 <= n <= 6:
                both(n - 2, 2)

        if n == 7:
            take_recv(q["g"].at[pl.ds(0, 7), :, 0], q["chips"][0])
        if n == 8:
            take_recv(q["g"].at[0, :, 0], q["chips"][1])

    def coarse_drain(q):
        g = q["g"]

        @pl.when(co == 0)
        def _():
            take_send(g.at[0, pl.ds(0, 3), 0], q["links"][0])
            take_send(g.at[pl.ds(0, 7), :, 0], q["links"][1])

        @pl.when(co == 1)
        def _():
            take_send(g.at[pl.ds(0, 7), 0, 0], q["links"][0])
            take_send(g.at[pl.ds(0, 3)], q["links"][1])

    def gather_copies(buf, order=(0, 1)):
        g = {"own": [], "opp": [], "fwd": [], "near": [], "far": [], "buf": buf}
        si = send_slot(buf.at[:, pl.ds(0, 3)])
        for s in order:
            near = slot(n_recv)
            far = slot(n_recv)
            g["near"].append(near)
            g["far"].append(far)
            g["own"].append(remote(buf.at[s, cr], buf.at[s, cr], sib, si, near))
            g["opp"].append([])
            for h in range(2):
                b = buf.at[s, cr, pl.ds(192 * h, 192)]
                g["opp"][-1].append(remote(b, b, opp, si, far))
            g["fwd"].append(remote(buf.at[s, oc], buf.at[s, oc], sib, si, near))
        return g

    def forward(g, s):
        take_recv(g["buf"].at[0, 0], g["far"][s])
        g["fwd"][s].start()

    def send(g, s):
        for c in g["opp"][s]:
            c.start()
        g["own"][s].start()

    def arrived(g, s):
        take_recv(g["buf"].at[0, pl.ds(0, 2)], g["near"][s])

    def combine():
        si = send_slot(pin)
        ri = slot(n_recv)
        for i, (half, dev) in enumerate(((1 - co, sib), (co, opp), (1 - co, ops))):
            remote(part.at[half], pin.at[i], dev, si, ri).start()
        return ri

    def solve_group(it, off):
        i = lax.rem(z + off, 8)
        x = rhs[it, i].reshape(768, 128)
        cols = pl.ds(pl.multiple_of(i * 768, 768), 768)
        return mm(km[:, cols], wide(x))

    def solve_most(it):
        def body(i, acc):
            return acc + solve_group(it, i + lax.div(i, 4))
        return lax.fori_loop(0, 7, body, jnp.zeros((96, 256), f32))

    def solve_rest(it, acc):
        co48[it, cr] = quad(acc + solve_group(it, 4), 48)
        si = send_slot(co48.at[it, pl.ds(0, 3)])
        ri = slot(n_recv)
        for dev in (opp, ops, sib):
            remote(co48.at[it, cr], co48.at[it, cr], dev, si, ri).start()
        return ri

    def weights(it, s):
        first = co48[it, pl.ds(2 * s, 2)].reshape(96, 128)
        hi, lo = split(first)
        zero = jnp.zeros((32, 128), bf16)
        left = jnp.concatenate([hi, zero, hi, zero], axis=0)
        right = jnp.concatenate([lo, zero, jnp.zeros((128, 128), bf16)], axis=0)
        return jnp.concatenate([left, right], axis=1)

    def rebuild(it, s):
        w = weights(it, s)

        def body(j, carry):
            rows = pl.ds(pl.multiple_of(j * 384, 384), 384)
            v = lb[it, s, j] + halves(mm(bt[s, rows, :], w))
            xs[s, rows, :] = wide(v)
            return carry
        lax.fori_loop(0, 4, body, 0)
        rows = pl.ds(pl.multiple_of(cr * 384, 384), 384)
        v = lb[it, s, cr] + halves(mm(bt[s, rows, :], w))
        if it == 0:
            vsum[s] = v
        else:
            out[0, s] = vsum[s] + v

    def pick(m, s, g):
        return halves(mm(pickm[m, 384 * g:384 * (g + 1)], xs[s]))

    ld_b.wait()
    for s in range(2):
        hi, lo = split(bf[s, cr, 0:96, :])
        bo[s, 0:96] = hi
        bo[s, 96:192] = lo
    ld_r.wait()
    for s in range(2):
        part[s] = quad(mm(bo[s], wide(rb[0, s, cr])), 96)
    for c in ld_i:
        c.wait()
    wanted = [-1, -2, 2, 3, 1 - co]
    for k in range(6):
        near = nbr[co, k] - 2 * d
        on = (cnt[co] > k).astype(jnp.int32)
        row = read_rows[k, pl.ds(co, 1), :]
        for a in range(5):
            h = (near == wanted[a]).astype(jnp.int32) * on
            lists[a, k:k + 1, :] = row * h + (h - 1)

    @pl.when(co == 0)
    def _():
        pl.semaphore_wait(bar, 12)

    @pl.when(co == 1)
    def _():
        pl.semaphore_wait(bar, 11)

    c_part = combine()
    s_list = send_slot(rl)
    r_list = slot(n_recv)
    c_list_dn = remote(lists.at[pl.ds(0, 2)], rl.at[0], dn, s_list, r_list)
    c_list_up = remote(lists.at[pl.ds(2, 2)], rl.at[1], up, s_list, r_list)
    s_b = send_slot(bf.at[:, pl.ds(0, 3), pl.ds(0, 96)])
    r_b = [slot(n_recv) for _ in range(3)]

    def basis(at, dev, ri):
        b = bf.at[at + (pl.ds(0, 96),)]
        return remote(b, b, dev, s_b, r_b[ri])

    c_b1 = basis((1 - cc, cr), otwin, 0)
    c_b2 = basis((cc, oc), twin, 1)
    c_bs = basis((slice(None), cr), sib, 2)
    c_bo = basis((slice(None), oc), sib, 2)
    c_b1.start()
    gr = gather_copies(rb.at[0])
    for s in range(2):
        send(gr, s)
    c_list_dn.start()
    c_list_up.start()
    c_bs.start()

    def zero_pad(j, carry):
        for s in range(2):
            bf[s, j, 96:128, :] = jnp.zeros((32, 384), f32)
        return carry
    lax.fori_loop(0, 4, zero_pad, 0)
    ld_l[0].wait()
    conv_matrix(0, 0)
    ld_s0 = load(6, s_hbm.at[0], stage.at[0])
    ld_l[1].wait()
    conv_matrix(0, 1)
    ld_s1 = load(7, s_hbm.at[1], stage.at[1])

    take_recv(pin, c_part)
    rhs[0, z, y, co] = (part[co] + pin[0]) + (pin[1] + pin[2])
    q = coarse_copies(0)
    coarse_step(q, 0)
    ld_k.wait()
    hi, lo = split(kst[...])
    km[0:48] = hi
    km[48:96] = lo
    take_recv(rl, r_list)
    build_pick(0, lambda k: rl[0, 0, pl.ds(k, 1), :])
    coarse_step(q, 1)
    build_pick(1, lambda k: rl[1, 0, pl.ds(k, 1), :])
    coarse_step(q, 2)
    forward(gr, 0)
    build_scatter(0)
    coarse_step(q, 3)
    gl = gather_copies(lb.at[0])
    arrived(gr, 0)
    for j in range(4):
        store_x(0, j, rb[0, 0, j])
    lb[0, 0, cr] = apply(0, 0)
    send(gl, 0)
    coarse_step(q, 4)
    c_b1.wait_recv()
    c_b2.start()
    build_pick(2, lambda k: rl[co, 1, pl.ds(k, 1), :])
    forward(gr, 1)
    coarse_step(q, 5)
    arrived(gr, 1)
    for j in range(4):
        store_x(1, j, rb[0, 1, j])
    lb[0, 1, cr] = apply(0, 1)
    gl["opp"][1][0].start()
    gl["own"][1].start()
    coarse_step(q, 7)
    acc = solve_most(0)
    coarse_step(q, 6)
    coarse_step(q, 8)
    cs = solve_rest(0, acc)
    gl["opp"][1][1].start()
    ld_s0.wait()
    conv_matrix(1, 0)
    ld_s1.wait()
    conv_matrix(1, 1)
    build_pick(3, lambda k: lists[4, pl.ds(k, 1), :])
    forward(gl, 0)
    c_b2.wait_recv()
    c_bo.start()
    build_scatter(1)
    take_recv(bf.at[:, pl.ds(0, 2), pl.ds(0, 96)], r_b[2])
    lax.fori_loop(0, 4, lambda j, carry: (build_bt(j), carry)[1], 0)
    for j in range(4):
        hi, lo = split(bf[co, j, 0:96, :])
        bw[0:96, 384 * j:384 * (j + 1)] = hi
        bw[96:192, 384 * j:384 * (j + 1)] = lo
    ld_c.wait()
    for k in range(6):
        hi, lo = split(cst[k])
        cm[k, 0:128] = hi
        cm[k, 128:256] = lo

    for it in range(ITERS):
        c_up = []
        c_dn = []
        s_ps = send_slot(ps.at[it])
        r_fr = []
        for g in range(2):
            part_rows = pl.ds(384 * g, 384)
            r_fr.append(slot(n_recv))
            c_up.append(remote(ps.at[it, 0, part_rows], fr.at[it, 0, part_rows], up, s_ps, r_fr[g]))
            c_dn.append(remote(ps.at[it, 1, part_rows], fr.at[it, 1, part_rows], dn, s_ps, r_fr[g]))
        if it == 1:
            arrived(gl, 0)
            arrived(gl, 1)
            for s in range(2):
                for j in range(4):
                    store_x(s, j, lb[1, s, j])
            for g in range(2):
                rows = slice(384 * g, 384 * (g + 1))
                ps[1, 1, rows] = pick(1, 0, g)
                ps[1, 0, rows] = pick(0, 1, g)
                ps[1, co, rows] = ps[1, co, rows] + pick(2, co, g)
                if g == 0:
                    take_recv(co48.at[it, pl.ds(0, 3)], cs)
                    ws = [weights(1, 1), weights(1, 0), weights(1, co)]
                for m, dest in ((0, 0), (1, 1), (2, co)):
                    ps[1, dest, rows] = ps[1, dest, rows] + halves(mm(qm[m, rows], ws[m]))
                c_up[g].start()
                c_dn[g].start()
            rebuild(1, 0)
            rebuild(1, 1)
        if it == 0:
            take_recv(co48.at[it, pl.ds(0, 3)], cs)
            arrived(gl, 0)
            rebuild(0, 0)
            forward(gl, 1)
            for g in range(2):
                rows = slice(384 * g, 384 * (g + 1))
                ps[0, 1, rows] = pick(1, 0, g)

                @pl.when(co == 0)
                def _():
                    c_dn[g].start()
            arrived(gl, 1)
            rebuild(0, 1)
            gy = gather_copies(rb.at[1])
            for g in range(2):
                rows = slice(384 * g, 384 * (g + 1))
                ps[0, 0, rows] = pick(0, 1, g)

                @pl.when(co == 1)
                def _():
                    c_up[g].start()
                ps[0, co, rows] = ps[0, co, rows] + pick(2, co, g)

                @pl.when(co == 0)
                def _():
                    c_up[g].start()

                @pl.when(co == 1)
                def _():
                    c_dn[g].start()
                rb[1, g, cr] = rb[0, g, cr] - damping * apply(1, g)
                send(gy, g)
        if it == 1:
            for s in range(2):
                res[s] = r1[s] - damping * apply(1, s)
        own_rows = [pick(3, 1 - co, g) for g in range(2)]
        s_tm = send_slot(tm.at[it, 0])
        r_tm = [slot(n_recv), slot(n_recv)]
        own = pl.ds(pl.multiple_of(cr * 384, 384), 384)
        for g in range(2):
            if it == 0:
                for m, src_s in ((0, 1), (1, 0)) if g == 0 else ((2, co),):
                    for h in range(2):
                        rows = slice(384 * h, 384 * (h + 1))
                        qm[m, rows] = mm(pickm[m, rows], bt[src_s]).astype(bf16)
            part_rows = pl.ds(384 * g, 384)
            if g == 1:
                take_recv(tm.at[it, 0, pl.ds(0, 384)], r_tm[0])
                early = [
                    halves(mm(tt[s, own, 0:384], wide(tm[it, s, 0:384]))) for s in range(2)
                ]
            take_recv(fr.at[it, :, part_rows], r_fr[g])
            src = own_rows[g] + fr[it, 0, part_rows] + fr[it, 1, part_rows]
            for k in range(3):
                rows = slice(384 * g + 128 * k, 384 * g + 128 * (k + 1))
                tm[it, co, rows, :] = quad(
                    mm(cm[3 * g + k], wide(src[128 * k:128 * (k + 1)])), 128
                )
            terms = tm.at[it, co, part_rows]
            remote(terms, terms, sib, s_tm, r_tm[g]).start()
            if it == 0:
                forward(gy, g)
        take_recv(tm.at[it, 0, pl.ds(0, 384)], r_tm[1])
        for s in range(2):
            late = halves(mm(tt[s, own, 384:768], wide(tm[it, s, 384:768])))
            own_inflow = early[s] + late
            if it == 0:
                r1[s] = rb[1, s, cr] + damping * own_inflow
                store_x(s, cr, r1[s])
            else:
                out[1, s] = 0.5 * (res[s] + damping * own_inflow)
        if it == 0:
            coarse_drain(q)
            gl = gather_copies(lb.at[1], (co, 1 - co))

            def fill(s):
                def body(i, carry):
                    j = lax.rem(cr + i, 4)
                    rows = pl.ds(pl.multiple_of(j * 384, 384), 384)
                    v = rb[1, s, j] + damping * halves(mm(tt[s, rows, :], wide(tm[0, s])))
                    xs[s, rows, :] = wide(v)
                    return carry
                lax.fori_loop(1, 4, body, 0)

            arrived(gy, 0)
            arrived(gy, 1)
            fill(co)
            rhs[1, z, y, co] = quad(mm(bw[...], xs[co]), 96)
            q = coarse_copies(1)
            coarse_step(q, 0)
            lb[1, co, cr] = apply(0, co)
            send(gl, 0)
            fill(1 - co)
            coarse_step(q, 1)
            lb[1, 1 - co, cr] = apply(0, 1 - co)
            send(gl, 1)
            coarse_step(q, 2)
            for n in range(3, 6):
                coarse_step(q, n)
            forward(gl, 0)
            coarse_step(q, 7)
            acc = solve_most(1)
            coarse_step(q, 6)
            forward(gl, 1)
            coarse_step(q, 8)
            cs = solve_rest(1, acc)
    coarse_drain(q)
    for ref, i in tail:
        take_send(ref, i)
    assert n_send[0] == N_SEND and n_recv[0] == N_RECV, (n_send, n_recv)


N_SEND = 19
N_RECV = 97


def per_device(
    load_cases,
    stiffness,
    local_inverse,
    coarse_basis,
    coarse_inverse,
    coupling,
    target_local_rows,
    neighbour_read_rows,
    neighbour,
    counts,
):
    any_spec = pl.BlockSpec(memory_space=pl.ANY)
    vmem = pl.BlockSpec(memory_space=pltpu.VMEM)
    V = pltpu.VMEM
    both = pl.pallas_call(
        kernel,
        name="schwarz",
        out_shape=jax.ShapeDtypeStruct((2, 2, 384, 128), f32),
        in_specs=[any_spec] * 10,
        out_specs=vmem,
        scratch_shapes=[
            V((2, 2, 4, 384, 128), f32),
            V((2, 2, 4, 384, 128), f32),
            V((2, 4, 128, 384), f32),
            V((2, 1536, 256), bf16),
            V((2, 192, 384), bf16),
            V((192, 1536), bf16),
            V((2, 2, 768, 1536), bf16),
            V((2, 384, 1536), f32),
            V((48, 6144), f32),
            V((96, 6144), bf16),
            V((2, 8, 4, 2, 96, 128), f32),
            V((2, 1536, 256), bf16),
            V((2, 384, 128), f32),
            V((2, 96, 128), f32),
            V((3, 96, 128), f32),
            V((4, 768, 1536), bf16),
            V((3, 768, 256), bf16),
            V((2, 1536, 768), bf16),
            V((2, 2, 768, 128), f32),
            V((2, 2, 768, 128), f32),
            V((2, 2, 768, 128), f32),
            V((6, 128, 128), f32),
            V((6, 256, 128), bf16),
            V((2, 2, 8, 128), jnp.int32),
            V((2, 4, 48, 128), f32),
            V((2, 384, 128), f32),
            V((2, 384, 128), f32),
            V((6, 2, 128), jnp.int32),
            V((6, 2, 128), jnp.int32),
            pltpu.SMEM((2, 6), jnp.int32),
            pltpu.SMEM((2,), jnp.int32),
            V((5, 8, 128), jnp.int32),
            pltpu.SemaphoreType.DMA((12,)),
            pltpu.SemaphoreType.DMA((N_SEND,)),
            pltpu.SemaphoreType.DMA((N_RECV,)),
        ],
        compiler_params=pltpu.CompilerParams(
            collective_id=0, has_side_effects=True, vmem_limit_bytes=66_000_000
        ),
    )(
        load_cases, stiffness, local_inverse, coarse_basis, coarse_inverse, coupling,
        target_local_rows.transpose(1, 0, 2), neighbour_read_rows.transpose(1, 0, 2),
        neighbour, counts,
    )
    return damping * both[0], 2.0 * both[1]


def solution(mesh):
    finer = Mesh(
        mesh.devices.reshape(8, 4, mesh.shape["crow"], mesh.shape["ccol"]),
        ("sub_0", "sub_1", "crow", "ccol"),
    )
    placed = (
        P(SUB, "crow", "ccol"),
        P(SUB, "crow", None),
        P(SUB, "crow", None),
        P(SUB, None, "crow"),
        P(SUB_CROW, None),
        P(SUB, None, None, None),
        P(SUB, None, None),
        P(SUB, None, None),
        P(SUB, None),
        P(SUB),
    )
    return jax.shard_map(
        per_device,
        mesh=finer,
        in_specs=placed,
        out_specs=(P(SUB, "crow", "ccol"), P(SUB, "crow", "ccol")),
        check_vma=False,
    )
```
